512 devices in a mesh: seq: 128 (over y, z, core), head: 4 (over x).
Axes of the slice: x: 4, y: 8, z: 8, core: 2. Of those that a mesh axis runs over, the one named last changes fastest.
Arguments:
- queries: bfloat16 [16384, 4096], P('seq', 'head'), may hold values from -6 to 6
- keys: bfloat16 [16384, 4096], P('seq', 'head'), may hold values from -6 to 6
- values: bfloat16 [16384, 4096], P('seq', 'head'), may hold values from -6 to 6
- hidden: bfloat16 [16384, 2048], P('seq', 'head'), may hold values from -6 to 6
- gate_weight: bfloat16 [2048, 256], P('head'), may hold values from -0.125 to 0.125
- level_slot: int32 [8], replicated, may hold values from 0 to 7, each once
- out_grad: bfloat16 [16384, 4096], P('seq', 'head'), may hold values from -6 to 6
Outputs:
- mixed: bfloat16 [16384, 4096], P('seq', 'head')
- grad_queries: bfloat16 [16384, 4096], P('seq', 'head')
- grad_keys: bfloat16 [16384, 4096], P('seq', 'head')
- grad_values: bfloat16 [16384, 4096], P('seq', 'head')
- grad_hidden: bfloat16 [16384, 2048], P('seq', 'head')
The draws below stay inside these ranges and needn't reach their ends.
Inputs may be any that keep to these rules, and one draw needn't show every extreme that they name: `level_slot`: each column index of a head's block appears once.
All inputs are finite; a program needn't handle non-finite values.
Results may differ from the reference program's by a relative error of at most 0.01.
Values may be sent and summed in bfloat16 or wider, within the bound.
No kernel may reach another device: no remote copies, remote signals or barrier semaphores. Data moves between devices by JAX's collectives and lax.ppermute only.
A program may use at most 64 MiB of HBM per device.

```python
import jax
import jax.numpy as jnp
from jax import lax

HEADS = 32
DK = 128
D = 2048
SPAN = 128
TOKENS = 16384
LEVELS = 8


def steps_of(key, dims, pieces, low, top_value):
    def one(dim, shards_of):
        heights = jax.random.uniform(jax.random.fold_in(jax.random.fold_in(key, 6), dim), (shards_of,), jnp.float32, low / len(pieces), top_value / len(pieces))
        return jnp.repeat(jnp.exp(heights), dims[dim] // shards_of).reshape((-1,) + (1,) * (len(dims) - dim - 1))

    level = one(*pieces[0])
    for cut in pieces[1:]:
        level = level * one(*cut)
    return level


def bell_draw(stream_key, dims, deviation, reach, cuts=(), kind=jnp.bfloat16):
    result = jax.random.normal(stream_key, dims, jnp.float32) * deviation
    if len(cuts) > 0:
        result = steps_of(stream_key, dims, cuts, -0.22, 0.18) * result
    return jnp.clip(result, min=-reach, max=reach).astype(kind)


def setup_inputs(seed: int = 0) -> dict:
    key_list = jax.random.split(jax.random.key(seed), 8)
    queries = bell_draw(key_list[0], (TOKENS, HEADS * DK), 1.0, 6.0, ((0, 128), (1, 4)))
    keys = bell_draw(key_list[1], (TOKENS, HEADS * DK), 1.0, 6.0, ((0, 128), (1, 4)))
    values = bell_draw(key_list[2], (TOKENS, HEADS * DK), 1.0, 6.0, ((0, 128), (1, 4)))
    hidden = bell_draw(key_list[3], (TOKENS, D), 1.0, 6.0, ((0, 128), (1, 4)))
    gate_weight = bell_draw(key_list[4], (D, HEADS * LEVELS), D ** -0.5, 0.125, ((0, 4),))
    level_slot = jax.random.permutation(key_list[5], LEVELS).astype(jnp.int32)
    out_grad = bell_draw(key_list[6], (TOKENS, HEADS * DK), 1.0, 6.0, ((0, 128), (1, 4)))
    return dict(queries=queries, keys=keys, values=values, hidden=hidden, gate_weight=gate_weight, level_slot=level_slot, out_grad=out_grad)


HIGH = lax.Precision.HIGHEST


def rounded(array):
    return lax.optimization_barrier(array.astype(jnp.bfloat16)).astype(jnp.float32)


def mix_head(items):
    query, key_part, value, grad, weight = items
    query = query.astype(jnp.float32)
    key_part = key_part.astype(jnp.float32)
    value = value.astype(jnp.float32)
    grad = grad.astype(jnp.float32)
    count = query.shape[0]
    position = jnp.arange(SPAN)
    causal = (position[:, None] >= position[None, :]).astype(jnp.float32)
    scores = jnp.einsum('ncd,nsd->ncs', query, key_part, precision=HIGH)
    attend = rounded(scores * causal / SPAN)
    intra = jnp.einsum('ncs,nse->nce', attend, value, precision=HIGH)
    states = jnp.einsum('ncd,nce->nde', key_part, value, precision=HIGH)
    mixed = weight[:, :, 0:1] * intra
    weight_grads = [jnp.sum(grad * intra, -1)]
    grad_query = jnp.zeros_like(query)
    state_grad = jnp.zeros_like(states)
    span_ids = jnp.arange(count, dtype=jnp.int32)
    for depth in range(1, LEVELS):
        shift_bits = depth - 1
        width = 1 << shift_bits
        blocks = states.reshape(count // width, width, DK, DK).sum(1)
        upper_bit = ((span_ids >> shift_bits) & 1)[:, None, None]
        below = blocks[jnp.maximum((span_ids >> shift_bits) - 1, 0).astype(jnp.int32)]
        level_state = rounded(jnp.where(upper_bit == 1, below, 0.0) / float(width * SPAN))
        level_out = jnp.einsum('ncd,nde->nce', query, level_state, precision=HIGH)
        level_weight = weight[:, :, depth:depth + 1]
        mixed = mixed + level_weight * level_out
        weight_grads.append(jnp.sum(grad * level_out, -1))
        grad_query = grad_query + level_weight * jnp.einsum('nce,nde->ncd', grad, level_state, precision=HIGH)
        weighted = rounded(level_weight * grad)
        level_grad = jnp.einsum('ncd,nce->nde', query, weighted, precision=HIGH)
        grad_blocks = level_grad.reshape(count // width, width, DK, DK).sum(1)
        above = grad_blocks[jnp.minimum((span_ids >> shift_bits) + 1, count // width - 1).astype(jnp.int32)]
        state_grad = state_grad + jnp.where(upper_bit == 0, above, 0.0) / float(width * SPAN)
    state_grad = rounded(state_grad)
    weighted_first = rounded(weight[:, :, 0:1] * grad)
    grad_score = rounded(jnp.einsum('nce,nse->ncs', weighted_first, value, precision=HIGH) * causal / SPAN)
    grad_query = grad_query + jnp.einsum('ncs,nsd->ncd', grad_score, key_part, precision=HIGH)
    grad_key = jnp.einsum('ncs,ncd->nsd', grad_score, query, precision=HIGH) + jnp.einsum('nce,nde->ncd', value, state_grad, precision=HIGH)
    grad_value = jnp.einsum('ncs,nce->nse', attend, weighted_first, precision=HIGH) + jnp.einsum('ncd,nde->nce', key_part, state_grad, precision=HIGH)
    return mixed, grad_query, grad_key, grad_value, jnp.stack(weight_grads, -1)


def reference(queries, keys, values, hidden, gate_weight, level_slot, out_grad):
    tokens = queries.shape[0]
    count = tokens // SPAN
    logits = jnp.dot(hidden, gate_weight, preferred_element_type=jnp.float32).reshape(tokens, HEADS, LEVELS)
    chosen = logits[:, :, level_slot.astype(jnp.int32)]
    weight = jax.nn.softplus(chosen)

    def split(array):
        return jnp.transpose(array.reshape(count, SPAN, HEADS, -1), (2, 0, 1, 3))

    def join(array):
        return jnp.transpose(array, (1, 2, 0, 3)).reshape(tokens, -1)

    mixed, grad_query, grad_key, grad_value, weight_grad = lax.map(
        mix_head, (split(queries), split(keys), split(values), split(out_grad), split(weight)))
    weight_grad = join(weight_grad).reshape(tokens, HEADS, LEVELS)
    chosen_grad = weight_grad * jax.nn.sigmoid(chosen)
    logit_grad = jnp.zeros_like(logits).at[:, :, level_slot.astype(jnp.int32)].set(chosen_grad)
    logit_grad = logit_grad.reshape(tokens, HEADS * LEVELS).astype(jnp.bfloat16)
    grad_hidden = jnp.dot(logit_grad, gate_weight.T, preferred_element_type=jnp.float32).astype(jnp.bfloat16)
    return (join(mixed).astype(jnp.bfloat16), join(grad_query).astype(jnp.bfloat16),
            join(grad_key).astype(jnp.bfloat16), join(grad_value).astype(jnp.bfloat16), grad_hidden)
```

```python
import jax
import jax.numpy as jnp
from jax import lax
from jax.experimental import pallas as pl
from jax.experimental.pallas import tpu as pltpu
from jax.sharding import Mesh, PartitionSpec as P

DK = 128
SPAN = 128
HALF = 4
LANES = HALF * DK
SLOTS = 6
BF = jnp.bfloat16
F32 = jnp.float32


def dot(a, b, ca, cb):
    return lax.dot_general(a, b, (((ca,), (cb,)), ((), ())), preferred_element_type=F32)


def vmem(n):
    return [pl.BlockSpec(memory_space=pltpu.VMEM)] * n


def anymem(n):
    return [pl.BlockSpec(memory_space=pl.ANY)] * n


def smem(n):
    return [pl.BlockSpec(memory_space=pltpu.SMEM)] * n


def shape(*dims, kind=BF):
    return jax.ShapeDtypeStruct(dims, kind)


def pack_body(meta, q, k, v, g, hidden, gate, send, own, partial, sems):
    core = meta[0]
    mine = pl.multiple_of(core * LANES, LANES)
    theirs = pl.multiple_of((1 - core) * LANES, LANES)
    copies = []
    for i, src in enumerate((q, k, v, g)):
        copies.append(pltpu.make_async_copy(src.at[:, pl.ds(theirs, LANES)], send.at[i], sems.at[i]))
        copies.append(pltpu.make_async_copy(src.at[:, pl.ds(mine, LANES)], own.at[i], sems.at[4 + i]))
    for copy in copies:
        copy.start()
    logits = dot(gate[...], hidden[...], 0, 1)
    for c in range(2):
        for x in range(4):
            row = x * 64 + c * 32
            partial[c * 4 + x] = logits[row : row + 32]
    for copy in copies:
        copy.wait()


def states_body(meta, slot, parts, own, other, up, cols, chosen, near_state, near_grad, rows):
    core, z, y = meta[0], meta[1], meta[2]
    for s in range(2):
        c = core if s == 0 else 1 - core
        logits = parts[c * 4] + parts[c * 4 + 1] + parts[c * 4 + 2] + parts[c * 4 + 3]
        rows[:, s * SPAN : (s + 1) * SPAN] = logits
    for h in range(HALF):
        for l in range(8):
            chosen[h * 8 + l : h * 8 + l + 1, :] = rows[pl.ds(h * 8 + slot[l], 1), :]
    x = chosen[...]
    weights = jnp.maximum(x, 0.0) + jnp.log1p(jnp.exp(-jnp.abs(x)))
    padded = jnp.concatenate([weights, jnp.zeros((128 - 8 * HALF, 2 * SPAN), F32)], 0)
    for s in range(2):
        cols[s] = jnp.transpose(padded[:, s * SPAN : (s + 1) * SPAN])
    both = jnp.concatenate([cols[0], cols[1]], 0)
    first = core == 0
    for h in range(HALF):
        lanes = slice(h * DK, (h + 1) * DK)
        q = jnp.concatenate([own[0, :, lanes], other[0, :, lanes]], 0)
        g = jnp.concatenate([own[3, :, lanes], other[3, :, lanes]], 0).astype(F32)
        state_own = dot(own[1, :, lanes], own[2, :, lanes], 0, 0)
        state_other = dot(other[1, :, lanes], other[2, :, lanes], 0, 0)
        state = state_own + state_other
        near_state[h] = (jnp.where(first, state_own, state_other) / SPAN).astype(BF)
        near = both[:, h * 8 + 1 : h * 8 + 2]
        near_g = (near * g).astype(BF)
        grad_own = dot(q[:SPAN], near_g[:SPAN], 0, 0)
        grad_other = dot(q[SPAN:], near_g[SPAN:], 0, 0)
        near_grad[h] = (jnp.where(first, grad_other, grad_own) / SPAN).astype(BF)
        weighted = jnp.concatenate(
            [(both[:, h * 8 + 2 + i : h * 8 + 3 + i] * g).astype(BF) for i in range(SLOTS)], 1
        )
        grads = dot(q, weighted, 0, 0)
        for i in range(SLOTS):
            bit = (z >> i) & 1 if i < 3 else (y >> (i - 3)) & 1
            piece = jnp.where(bit == 1, grads[:, i * DK : (i + 1) * DK], state).astype(BF)
            up[2 * h, i] = piece[:64]
            up[2 * h + 1, i] = piece[64:]


def local_body(meta, own, other, cols, near_state, near_grad, part, sums):
    core = meta[0]
    at = lax.broadcasted_iota(jnp.int32, (SPAN, SPAN), 0)
    to = lax.broadcasted_iota(jnp.int32, (SPAN, SPAN), 1)
    causal = at >= to
    for s, src in enumerate((own, other)):
        upper = (core == 1) if s == 0 else (core == 0)
        total = jnp.zeros((SPAN, 128), F32)
        weights = cols[s]
        for h in range(HALF):
            lanes = slice(h * DK, (h + 1) * DK)
            q, k, v, g = (src[i, :, lanes] for i in range(4))
            gf = g.astype(F32)
            w0 = weights[:, h * 8 : h * 8 + 1]
            w1 = weights[:, h * 8 + 1 : h * 8 + 2]
            g0 = (w0 * gf).astype(BF)
            g1 = (w1 * gf).astype(BF)
            attend = jnp.where(causal, dot(q, k, 1, 1) / SPAN, 0.0).astype(BF)
            score = jnp.where(causal, dot(g0, v, 1, 1) / SPAN, 0.0).astype(BF)
            intra = dot(attend, v, 1, 0)
            zero = jnp.zeros((DK, DK), BF)
            level = jnp.where(upper, near_state[h], zero)
            back = jnp.where(upper, zero, near_grad[h])
            near = dot(q, level, 1, 0)
            part[s, 0, :, lanes] = w0 * intra + w1 * near
            part[s, 1, :, lanes] = dot(score, k, 1, 0) + dot(g1, level, 1, 1)
            part[s, 2, :, lanes] = dot(score, q, 0, 0) + dot(v, back, 1, 1)
            part[s, 3, :, lanes] = dot(attend, g0, 0, 0) + dot(k, back, 1, 0)
            total = jnp.where(to == h * 8, jnp.sum(gf * intra, -1, keepdims=True), total)
            total = jnp.where(to == h * 8 + 1, jnp.sum(gf * near, -1, keepdims=True), total)
        sums[s] = total


def along_z_body(meta, got, send):
    y = meta[2]
    totals = []
    for i in range(3, SLOTS):
        total = got[0, i].astype(F32)
        for z in range(1, 8):
            total = total + got[z, i].astype(F32)
        totals.append(total.astype(BF))
    send[y] = jnp.zeros_like(totals[0])
    for step in range(1, 8):
        send[y ^ step] = totals[step.bit_length() - 1]


def buckets_body(meta, got, from_y, down):
    y = meta[2]
    for i in range(3):
        width = 1 << i
        scale = 1.0 / (2 * width * SPAN)
        for block in range(8 // width):
            total = got[block * width, i].astype(F32)
            for z in range(block * width + 1, (block + 1) * width):
                total = total + got[z, i].astype(F32)
            total = (total * scale).astype(BF)
            target = block ^ 1
            for z in range(target * width, (target + 1) * width):
                down[z, i] = total
    for i in range(3):
        width = 1 << i
        scale = 1.0 / (16 * width * SPAN)
        total = from_y[y ^ width].astype(F32)
        for step in range(width + 1, 2 * width):
            total = total + from_y[y ^ step].astype(F32)
        total = (total * scale).astype(BF)
        for z in range(8):
            down[z, 3 + i] = total


def final_body(meta, slot, own, other, cols, chosen, part, sums, got, keep, send, logit_grad, rows):
    core, z, y = meta[0], meta[1], meta[2]
    lane = lax.broadcasted_iota(jnp.int32, (2 * SPAN, 128), 1)
    both = jnp.concatenate([cols[0], cols[1]], 0)
    total = jnp.concatenate([sums[0], sums[1]], 0)
    for h in range(HALF):
        lanes = slice(h * DK, (h + 1) * DK)
        q, k, v, g = (
            jnp.concatenate([own[i, :, lanes], other[i, :, lanes]], 0) for i in range(4)
        )
        gf = g.astype(F32)
        levels = []
        back = jnp.zeros((DK, DK), F32)
        for i in range(SLOTS):
            bit = (z >> i) & 1 if i < 3 else (y >> (i - 3)) & 1
            state = jnp.concatenate([got[2 * h, i], got[2 * h + 1, i]], 0)
            zero = jnp.zeros_like(state)
            levels.append(jnp.where(bit == 1, state, zero))
            back = back + jnp.where(bit == 1, zero, state).astype(F32)
        back = back.astype(BF)
        levels = jnp.concatenate(levels, 1)
        outs = dot(q, levels, 1, 0)
        mixed = jnp.concatenate([part[0, 0, :, lanes], part[1, 0, :, lanes]], 0)
        weighted = []
        for i in range(SLOTS):
            w = both[:, h * 8 + 2 + i : h * 8 + 3 + i]
            out = outs[:, i * DK : (i + 1) * DK]
            mixed = mixed + w * out
            weighted.append((w * gf).astype(BF))
            total = jnp.where(lane == h * 8 + 2 + i, jnp.sum(gf * out, -1, keepdims=True), total)
        dq = dot(jnp.concatenate(weighted, 1), levels, 1, 1)
        dk = dot(v, back, 1, 1)
        dv = dot(k, back, 1, 0)
        for s, dst in enumerate((keep, send)):
            span = slice(s * SPAN, (s + 1) * SPAN)
            dst[0, :, lanes] = mixed[span].astype(BF)
            dst[1, :, lanes] = (part[s, 1, :, lanes] + dq[span]).astype(BF)
            dst[2, :, lanes] = (part[s, 2, :, lanes] + dk[span]).astype(BF)
            dst[3, :, lanes] = (part[s, 3, :, lanes] + dv[span]).astype(BF)
    for s in range(2):
        c = core if s == 0 else 1 - core
        by_level = jnp.transpose(total[s * SPAN : (s + 1) * SPAN])[: 8 * HALF]
        by_level = by_level * jax.nn.sigmoid(chosen[:, s * SPAN : (s + 1) * SPAN])
        for h in range(HALF):
            for l in range(8):
                rows[pl.ds(h * 8 + slot[l], 1), :] = by_level[h * 8 + l : h * 8 + l + 1, :]
        ready = rows[...].astype(BF)
        for x in range(4):
            logit_grad[c * 4 + x] = ready


def unpack_body(meta, keep, got, logit_grad, gate, mixed, dq, dk, dv, dhidden, sems):
    core = meta[0]
    mine = pl.multiple_of(core * LANES, LANES)
    theirs = pl.multiple_of((1 - core) * LANES, LANES)
    copies = []
    for i, dst in enumerate((mixed, dq, dk, dv)):
        copies.append(pltpu.make_async_copy(keep.at[i], dst.at[:, pl.ds(mine, LANES)], sems.at[i]))
        copies.append(pltpu.make_async_copy(got.at[i], dst.at[:, pl.ds(theirs, LANES)], sems.at[4 + i]))
    for copy in copies:
        copy.start()
    grads = jnp.concatenate([logit_grad[c * 4 + x] for x in range(4) for c in range(2)], 0)
    dhidden[...] = dot(grads, gate[...], 0, 1).astype(BF)
    for copy in copies:
        copy.wait()


def local(queries, keys, values, hidden, gate_weight, level_slot, out_grad):
    core, z, y = lax.axis_index("core"), lax.axis_index("z"), lax.axis_index("y")
    meta = jnp.stack([core, z, y]).astype(jnp.int32)
    swap = [(0, 1), (1, 0)]

    def exchange(array, axis):
        return lax.all_to_all(array, axis, 0, 0, tiled=True)

    send, own, partial = pl.pallas_call(
        pack_body,
        out_shape=(shape(4, SPAN, LANES), shape(4, SPAN, LANES), shape(8, 32, SPAN, kind=F32)),
        in_specs=smem(1) + anymem(4) + vmem(2),
        out_specs=tuple(anymem(2) + vmem(1)),
        scratch_shapes=[pltpu.SemaphoreType.DMA((8,))],
        name="pack",
    )(meta, queries, keys, values, out_grad, hidden, gate_weight)
    other = lax.ppermute(send, "core", swap)
    parts = exchange(partial, ("core", "head"))
    up, cols, chosen, near_state, near_grad = pl.pallas_call(
        states_body,
        out_shape=(
            shape(8, SLOTS, 64, DK),
            shape(2, SPAN, 128, kind=F32),
            shape(8 * HALF, 2 * SPAN, kind=F32),
            shape(HALF, DK, DK),
            shape(HALF, DK, DK),
        ),
        in_specs=smem(2) + vmem(3),
        out_specs=tuple(vmem(5)),
        scratch_shapes=[pltpu.VMEM((8 * HALF, 2 * SPAN), F32)],
        name="states",
    )(meta, level_slot, parts, own, other)
    got = exchange(up, "z")
    part, sums = pl.pallas_call(
        local_body,
        out_shape=(shape(2, 4, SPAN, LANES, kind=F32), shape(2, SPAN, 128, kind=F32)),
        in_specs=smem(1) + vmem(5),
        out_specs=tuple(vmem(2)),
        name="local",
    )(meta, own, other, cols, near_state, near_grad)
    to_y = pl.pallas_call(
        along_z_body,
        out_shape=shape(8, 64, DK),
        in_specs=smem(1) + vmem(1),
        out_specs=vmem(1)[0],
        name="along_z",
    )(meta, got)
    from_y = exchange(to_y, "y")
    down = pl.pallas_call(
        buckets_body,
        out_shape=shape(8, SLOTS, 64, DK),
        in_specs=smem(1) + vmem(2),
        out_specs=vmem(1)[0],
        name="buckets",
    )(meta, got, from_y)
    sums_here = exchange(down, "z")
    keep, away, logit_grad = pl.pallas_call(
        final_body,
        out_shape=(shape(4, SPAN, LANES), shape(4, SPAN, LANES), shape(8, 8 * HALF, SPAN)),
        in_specs=smem(2) + vmem(7),
        out_specs=tuple(vmem(3)),
        scratch_shapes=[pltpu.VMEM((8 * HALF, SPAN), F32)],
        name="final",
    )(meta, level_slot, own, other, cols, chosen, part, sums, sums_here)
    back = lax.ppermute(away, "core", swap)
    all_grads = exchange(logit_grad, ("core", "head"))
    return pl.pallas_call(
        unpack_body,
        out_shape=(shape(SPAN, 2 * LANES),) * 4 + (shape(SPAN, hidden.shape[1]),),
        in_specs=smem(1) + anymem(2) + vmem(2),
        out_specs=tuple(anymem(4) + vmem(1)),
        scratch_shapes=[pltpu.SemaphoreType.DMA((8,))],
        name="unpack",
    )(meta, keep, back, all_grads, gate_weight)


def solution(mesh):
    names = ("y", "z", "core", "head")
    fine = Mesh(mesh.devices.reshape(8, 8, 2, 4), names)
    tokens = ("y", "z", "core")
    rows = P(tokens, "head")
    return jax.shard_map(
        local,
        mesh=fine,
        in_specs=(rows, rows, rows, rows, P("head", None), P(), rows),
        out_specs=(rows,) * 5,
        check_vma=False,
    )
```

```python
import jax
import jax.numpy as jnp
from jax import lax
from jax.experimental import pallas as pl
from jax.experimental.pallas import tpu as pltpu
from jax.sharding import Mesh, PartitionSpec as P

DK = 128
SPAN = 128
HALF = 4
LANES = HALF * DK
SLOTS = 6
BF = jnp.bfloat16
F32 = jnp.float32


def dot(a, b, ca, cb):
    return lax.dot_general(a, b, (((ca,), (cb,)), ((), ())), preferred_element_type=F32)


def vmem(n):
    return [pl.BlockSpec(memory_space=pltpu.VMEM)] * n


def anymem(n):
    return [pl.BlockSpec(memory_space=pl.ANY)] * n


def smem(n):
    return [pl.BlockSpec(memory_space=pltpu.SMEM)] * n


def shape(*dims, kind=BF):
    return pltpu.VMEM(dims, kind)


def near(*arrays):
    return [pltpu.with_memory_space_constraint(a, pltpu.VMEM) for a in arrays]


SMALL = pltpu.CompilerParams(vmem_limit_bytes=16 << 20)


def pack_body(meta, q, k, v, g, hidden, gate, send, own, partial):
    first = meta[0] == 0
    for i, src in enumerate((q, k, v, g)):
        low, high = src[:, :LANES], src[:, LANES:]
        own[i] = jnp.where(first, low, high)
        send[i] = jnp.where(first, high, low)
    logits = dot(gate[...], hidden[...], 0, 1)
    for c in range(2):
        for x in range(4):
            row = x * 64 + c * 32
            partial[c * 4 + x] = logits[row : row + 32]


def states_body(meta, slot, parts, own, other, up, cols, chosen, near_state, near_grad, rows):
    core, z, y = meta[0], meta[1], meta[2]
    for s in range(2):
        c = core if s == 0 else 1 - core
        logits = parts[c * 4] + parts[c * 4 + 1] + parts[c * 4 + 2] + parts[c * 4 + 3]
        rows[:, s * SPAN : (s + 1) * SPAN] = logits
    for h in range(HALF):
        for l in range(8):
            chosen[h * 8 + l : h * 8 + l + 1, :] = rows[pl.ds(h * 8 + slot[l], 1), :]
    x = chosen[...]
    weights = jnp.maximum(x, 0.0) + jnp.log1p(jnp.exp(-jnp.abs(x)))
    padded = jnp.concatenate([weights, jnp.zeros((128 - 8 * HALF, 2 * SPAN), F32)], 0)
    for s in range(2):
        cols[s] = jnp.transpose(padded[:, s * SPAN : (s + 1) * SPAN])
    both = jnp.concatenate([cols[0], cols[1]], 0)
    first = core == 0
    for h in range(HALF):
        lanes = slice(h * DK, (h + 1) * DK)
        q = jnp.concatenate([own[0, :, lanes], other[0, :, lanes]], 0)
        g = jnp.concatenate([own[3, :, lanes], other[3, :, lanes]], 0).astype(F32)
        state_own = dot(own[1, :, lanes], own[2, :, lanes], 0, 0)
        state_other = dot(other[1, :, lanes], other[2, :, lanes], 0, 0)
        state = state_own + state_other
        near_state[h] = (jnp.where(first, state_own, state_other) / SPAN).astype(BF)
        near = both[:, h * 8 + 1 : h * 8 + 2]
        near_g = (near * g).astype(BF)
        grad_own = dot(q[:SPAN], near_g[:SPAN], 0, 0)
        grad_other = dot(q[SPAN:], near_g[SPAN:], 0, 0)
        near_grad[h] = (jnp.where(first, grad_other, grad_own) / SPAN).astype(BF)
        weighted = jnp.concatenate(
            [(both[:, h * 8 + 2 + i : h * 8 + 3 + i] * g).astype(BF) for i in range(SLOTS)], 1
        )
        grads = dot(q, weighted, 0, 0)
        for i in range(SLOTS):
            bit = (z >> i) & 1 if i < 3 else (y >> (i - 3)) & 1
            piece = jnp.where(bit == 1, grads[:, i * DK : (i + 1) * DK], state).astype(BF)
            up[2 * h, i] = piece[:64]
            up[2 * h + 1, i] = piece[64:]


def local_body(meta, own, other, cols, near_state, near_grad, part, sums):
    core = meta[0]
    at = lax.broadcasted_iota(jnp.int32, (SPAN, SPAN), 0)
    to = lax.broadcasted_iota(jnp.int32, (SPAN, SPAN), 1)
    causal = at >= to
    for s, src in enumerate((own, other)):
        upper = (core == 1) if s == 0 else (core == 0)
        total = jnp.zeros((SPAN, 128), F32)
        weights = cols[s]
        for h in range(HALF):
            lanes = slice(h * DK, (h + 1) * DK)
            q, k, v, g = (src[i, :, lanes] for i in range(4))
            gf = g.astype(F32)
            w0 = weights[:, h * 8 : h * 8 + 1]
            w1 = weights[:, h * 8 + 1 : h * 8 + 2]
            g0 = (w0 * gf).astype(BF)
            g1 = (w1 * gf).astype(BF)
            attend = jnp.where(causal, dot(q, k, 1, 1) / SPAN, 0.0).astype(BF)
            score = jnp.where(causal, dot(g0, v, 1, 1) / SPAN, 0.0).astype(BF)
            intra = dot(attend, v, 1, 0)
            zero = jnp.zeros((DK, DK), BF)
            level = jnp.where(upper, near_state[h], zero)
            back = jnp.where(upper, zero, near_grad[h])
            near = dot(q, level, 1, 0)
            part[s, 0, :, lanes] = w0 * intra + w1 * near
            part[s, 1, :, lanes] = dot(score, k, 1, 0) + dot(g1, level, 1, 1)
            part[s, 2, :, lanes] = dot(score, q, 0, 0) + dot(v, back, 1, 1)
            part[s, 3, :, lanes] = dot(attend, g0, 0, 0) + dot(k, back, 1, 0)
            total = jnp.where(to == h * 8, jnp.sum(gf * intra, -1, keepdims=True), total)
            total = jnp.where(to == h * 8 + 1, jnp.sum(gf * near, -1, keepdims=True), total)
        sums[s] = total


def along_z_body(meta, got, send):
    y = meta[2]
    totals = []
    for i in range(3, SLOTS):
        total = got[0, i].astype(F32)
        for z in range(1, 8):
            total = total + got[z, i].astype(F32)
        totals.append(total.astype(BF))
    send[y] = jnp.zeros_like(totals[0])
    for step in range(1, 8):
        send[y ^ step] = totals[step.bit_length() - 1]


def buckets_body(meta, got, from_y, down):
    y = meta[2]
    for i in range(3):
        width = 1 << i
        scale = 1.0 / (2 * width * SPAN)
        for block in range(8 // width):
            total = got[block * width, i].astype(F32)
            for z in range(block * width + 1, (block + 1) * width):
                total = total + got[z, i].astype(F32)
            total = (total * scale).astype(BF)
            target = block ^ 1
            for z in range(target * width, (target + 1) * width):
                down[z, i] = total
    for i in range(3):
        width = 1 << i
        scale = 1.0 / (16 * width * SPAN)
        total = from_y[y ^ width].astype(F32)
        for step in range(width + 1, 2 * width):
            total = total + from_y[y ^ step].astype(F32)
        total = (total * scale).astype(BF)
        for z in range(8):
            down[z, 3 + i] = total


def final_body(meta, slot, own, other, cols, chosen, part, sums, got, keep, send, logit_grad, rows):
    core, z, y = meta[0], meta[1], meta[2]
    lane = lax.broadcasted_iota(jnp.int32, (2 * SPAN, 128), 1)
    both = jnp.concatenate([cols[0], cols[1]], 0)
    total = jnp.concatenate([sums[0], sums[1]], 0)
    for h in range(HALF):
        lanes = slice(h * DK, (h + 1) * DK)
        q, k, v, g = (
            jnp.concatenate([own[i, :, lanes], other[i, :, lanes]], 0) for i in range(4)
        )
        gf = g.astype(F32)
        levels = []
        back = jnp.zeros((DK, DK), F32)
        for i in range(SLOTS):
            bit = (z >> i) & 1 if i < 3 else (y >> (i - 3)) & 1
            state = jnp.concatenate([got[2 * h, i], got[2 * h + 1, i]], 0)
            zero = jnp.zeros_like(state)
            levels.append(jnp.where(bit == 1, state, zero))
            back = back + jnp.where(bit == 1, zero, state).astype(F32)
        back = back.astype(BF)
        levels = jnp.concatenate(levels, 1)
        outs = dot(q, levels, 1, 0)
        mixed = jnp.concatenate([part[0, 0, :, lanes], part[1, 0, :, lanes]], 0)
        weighted = []
        for i in range(SLOTS):
            w = both[:, h * 8 + 2 + i : h * 8 + 3 + i]
            out = outs[:, i * DK : (i + 1) * DK]
            mixed = mixed + w * out
            weighted.append((w * gf).astype(BF))
            total = jnp.where(lane == h * 8 + 2 + i, jnp.sum(gf * out, -1, keepdims=True), total)
        dq = dot(jnp.concatenate(weighted, 1), levels, 1, 1)
        dk = dot(v, back, 1, 1)
        dv = dot(k, back, 1, 0)
        for s, dst in enumerate((keep, send)):
            span = slice(s * SPAN, (s + 1) * SPAN)
            dst[0, :, lanes] = mixed[span].astype(BF)
            dst[1, :, lanes] = (part[s, 1, :, lanes] + dq[span]).astype(BF)
            dst[2, :, lanes] = (part[s, 2, :, lanes] + dk[span]).astype(BF)
            dst[3, :, lanes] = (part[s, 3, :, lanes] + dv[span]).astype(BF)
    for s in range(2):
        c = core if s == 0 else 1 - core
        by_level = jnp.transpose(total[s * SPAN : (s + 1) * SPAN])[: 8 * HALF]
        by_level = by_level * jax.nn.sigmoid(chosen[:, s * SPAN : (s + 1) * SPAN])
        for h in range(HALF):
            for l in range(8):
                rows[pl.ds(h * 8 + slot[l], 1), :] = by_level[h * 8 + l : h * 8 + l + 1, :]
        ready = rows[...].astype(BF)
        for x in range(4):
            logit_grad[c * 4 + x] = ready


def unpack_body(meta, keep, got, logit_grad, gate, mixed, dq, dk, dv, dhidden):
    first = meta[0] == 0
    for i, dst in enumerate((mixed, dq, dk, dv)):
        here, there = keep[i], got[i]
        dst[:, :LANES] = jnp.where(first, here, there)
        dst[:, LANES:] = jnp.where(first, there, here)
    grads = jnp.concatenate([logit_grad[c * 4 + x] for x in range(4) for c in range(2)], 0)
    dhidden[...] = dot(grads, gate[...], 0, 1).astype(BF)


def local(queries, keys, values, hidden, gate_weight, level_slot, out_grad):
    core, z, y = lax.axis_index("core"), lax.axis_index("z"), lax.axis_index("y")
    meta = jnp.stack([core, z, y]).astype(jnp.int32)
    swap = [(0, 1), (1, 0)]

    def exchange(array, axis):
        return lax.all_to_all(array, axis, 0, 0, tiled=True)

    send, own, partial = pl.pallas_call(
        pack_body,
        out_shape=(shape(4, SPAN, LANES), shape(4, SPAN, LANES), shape(8, 32, SPAN, kind=F32)),
        in_specs=smem(1) + vmem(6),
        out_specs=tuple(vmem(3)),
        compiler_params=SMALL,
        name="pack",
    )(meta, queries, keys, values, out_grad, hidden, gate_weight)
    other = lax.ppermute(send, "core", swap)
    parts = exchange(partial, ("core", "head"))
    up, cols, chosen, near_state, near_grad = pl.pallas_call(
        states_body,
        out_shape=(
            shape(8, SLOTS, 64, DK),
            shape(2, SPAN, 128, kind=F32),
            shape(8 * HALF, 2 * SPAN, kind=F32),
            shape(HALF, DK, DK),
            shape(HALF, DK, DK),
        ),
        in_specs=smem(2) + vmem(3),
        out_specs=tuple(vmem(5)),
        scratch_shapes=[pltpu.VMEM((8 * HALF, 2 * SPAN), F32)],
        compiler_params=SMALL,
        name="states",
    )(meta, level_slot, *near(parts, own, other))
    got = exchange(up, "z")
    part, sums = pl.pallas_call(
        local_body,
        out_shape=(shape(2, 4, SPAN, LANES, kind=F32), shape(2, SPAN, 128, kind=F32)),
        in_specs=smem(1) + vmem(5),
        out_specs=tuple(vmem(2)),
        compiler_params=SMALL,
        name="local",
    )(meta, *near(own, other, cols, near_state, near_grad))
    to_y = pl.pallas_call(
        along_z_body,
        out_shape=shape(8, 64, DK),
        in_specs=smem(1) + vmem(1),
        out_specs=vmem(1)[0],
        compiler_params=SMALL,
        name="along_z",
    )(meta, *near(got))
    from_y = exchange(to_y, "y")
    down = pl.pallas_call(
        buckets_body,
        out_shape=shape(8, SLOTS, 64, DK),
        in_specs=smem(1) + vmem(2),
        out_specs=vmem(1)[0],
        compiler_params=SMALL,
        name="buckets",
    )(meta, *near(got, from_y))
    sums_here = exchange(down, "z")
    keep, away, logit_grad = pl.pallas_call(
        final_body,
        out_shape=(shape(4, SPAN, LANES), shape(4, SPAN, LANES), shape(8, 8 * HALF, SPAN)),
        in_specs=smem(2) + vmem(7),
        out_specs=tuple(vmem(3)),
        scratch_shapes=[pltpu.VMEM((8 * HALF, SPAN), F32)],
        compiler_params=SMALL,
        name="final",
    )(meta, level_slot, *near(own, other, cols, chosen, part, sums, sums_here))
    back = lax.ppermute(away, "core", swap)
    all_grads = exchange(logit_grad, ("core", "head"))
    outs = (jax.ShapeDtypeStruct((SPAN, 2 * LANES), BF),) * 4
    return pl.pallas_call(
        unpack_body,
        out_shape=outs + (jax.ShapeDtypeStruct((SPAN, hidden.shape[1]), BF),),
        in_specs=smem(1) + vmem(4),
        out_specs=tuple(vmem(5)),
        compiler_params=SMALL,
        name="unpack",
    )(meta, *near(keep, back, all_grads), gate_weight)


def solution(mesh):
    names = ("y", "z", "core", "head")
    fine = Mesh(mesh.devices.reshape(8, 8, 2, 4), names)
    tokens = ("y", "z", "core")
    rows = P(tokens, "head")
    return jax.shard_map(
        local,
        mesh=fine,
        in_specs=(rows, rows, rows, rows, P("head", None), P(), rows),
        out_specs=(rows,) * 5,
        check_vma=False,
    )
```

```python
import jax
import jax.numpy as jnp
from jax import lax
from jax.experimental import pallas as pl
from jax.experimental.pallas import tpu as pltpu
from jax.sharding import Mesh, PartitionSpec as P


DK = 128
SPAN = 128
HALF = 4
LANES = HALF * DK
SLOTS = 6
BF = jnp.bfloat16
F32 = jnp.float32


def dot(a, b, ca, cb):
    return lax.dot_general(a, b, (((ca,), (cb,)), ((), ())), preferred_element_type=F32)


def vmem(n):
    return [pl.BlockSpec(memory_space=pltpu.VMEM)] * n


def hbm(n):
    return [pl.BlockSpec(memory_space=pltpu.HBM)] * n


def smem(n):
    return [pl.BlockSpec(memory_space=pltpu.SMEM)] * n


def shape(*dims, kind=BF):
    return pltpu.VMEM(dims, kind)


def near(*arrays):
    return [pltpu.with_memory_space_constraint(a, pltpu.VMEM) for a in arrays]


def far(*arrays):
    return [pltpu.with_memory_space_constraint(a, pltpu.HBM) for a in arrays]


SMALL = pltpu.CompilerParams(vmem_limit_bytes=16 << 20)


def pack_body(meta, q, k, v, g, hidden, gate, send, own, partial, held, held_hidden, held_gate, sems):
    copies = [
        pltpu.make_async_copy(hidden, held_hidden, sems.at[0]),
        pltpu.make_async_copy(gate.at[:256], held_gate.at[:256], sems.at[1]),
        pltpu.make_async_copy(gate.at[256:], held_gate.at[256:], sems.at[2]),
    ]
    for i, src in enumerate((q, k, v, g)):
        for part in range(2):
            rows = slice(part * 64, part * 64 + 64)
            copies.append(
                pltpu.make_async_copy(src.at[rows], held.at[i, rows], sems.at[3 + 2 * i + part])
            )
    for copy in copies:
        copy.start()
    for copy in copies[:3]:
        copy.wait()
    logits = dot(held_gate[...], held_hidden[...], 0, 1)
    for c in range(2):
        for x in range(4):
            row = x * 64 + c * 32
            partial[c * 4 + x] = logits[row : row + 32]
    first = meta[0] == 0
    for i in range(4):
        copies[3 + 2 * i].wait()
        copies[4 + 2 * i].wait()
        low, high = held[i, :, :LANES], held[i, :, LANES:]
        own[i] = jnp.where(first, low, high)
        send[i] = jnp.where(first, high, low)


def states_body(meta, parts, own, other, up, cols, chosen, near_state, near_grad, rows):
    core, z, y = meta[0], meta[1], meta[2]
    for s in range(2):
        c = core if s == 0 else 1 - core
        logits = parts[c * 4] + parts[c * 4 + 1] + parts[c * 4 + 2] + parts[c * 4 + 3]
        rows[:, s * SPAN : (s + 1) * SPAN] = logits
    for h in range(HALF):
        for l in range(8):
            chosen[h * 8 + l : h * 8 + l + 1, :] = rows[pl.ds(h * 8 + meta[3 + l], 1), :]
    x = chosen[...]
    weights = jnp.maximum(x, 0.0) + jnp.log1p(jnp.exp(-jnp.abs(x)))
    padded = jnp.concatenate([weights, jnp.zeros((128 - 8 * HALF, 2 * SPAN), F32)], 0)
    for s in range(2):
        cols[s] = jnp.transpose(padded[:, s * SPAN : (s + 1) * SPAN])
    both = jnp.concatenate([cols[0], cols[1]], 0)
    first = core == 0
    for h in range(HALF):
        lanes = slice(h * DK, (h + 1) * DK)
        q = jnp.concatenate([own[0, :, lanes], other[0, :, lanes]], 0)
        g = jnp.concatenate([own[3, :, lanes], other[3, :, lanes]], 0).astype(F32)
        state_own = dot(own[1, :, lanes], own[2, :, lanes], 0, 0)
        state_other = dot(other[1, :, lanes], other[2, :, lanes], 0, 0)
        state = state_own + state_other
        near_state[h] = (jnp.where(first, state_own, state_other) / SPAN).astype(BF)
        near = both[:, h * 8 + 1 : h * 8 + 2]
        near_g = (near * g).astype(BF)
        grad_own = dot(q[:SPAN], near_g[:SPAN], 0, 0)
        grad_other = dot(q[SPAN:], near_g[SPAN:], 0, 0)
        near_grad[h] = (jnp.where(first, grad_other, grad_own) / SPAN).astype(BF)
        weighted = jnp.concatenate(
            [(both[:, h * 8 + 2 + i : h * 8 + 3 + i] * g).astype(BF) for i in range(SLOTS)], 1
        )
        grads = dot(q, weighted, 0, 0)
        for i in range(SLOTS):
            bit = (z >> i) & 1 if i < 3 else (y >> (i - 3)) & 1
            piece = jnp.where(bit == 1, grads[:, i * DK : (i + 1) * DK], state).astype(BF)
            up[2 * h, i] = piece[:64]
            up[2 * h + 1, i] = piece[64:]


def local_body(meta, own, other, cols, near_state, near_grad, part_own, part_other, sums):
    core = meta[0]
    at = lax.broadcasted_iota(jnp.int32, (SPAN, SPAN), 0)
    to = lax.broadcasted_iota(jnp.int32, (SPAN, SPAN), 1)
    causal = at >= to
    for s, (src, part) in enumerate(((own, part_own), (other, part_other))):
        upper = (core == 1) if s == 0 else (core == 0)
        total = jnp.zeros((SPAN, 128), F32)
        weights = cols[s]
        for h in range(HALF):
            lanes = slice(h * DK, (h + 1) * DK)
            q, k, v, g = (src[i, :, lanes] for i in range(4))
            gf = g.astype(F32)
            w0 = weights[:, h * 8 : h * 8 + 1]
            w1 = weights[:, h * 8 + 1 : h * 8 + 2]
            g0 = (w0 * gf).astype(BF)
            g1 = (w1 * gf).astype(BF)
            attend = jnp.where(causal, dot(q, k, 1, 1) / SPAN, 0.0).astype(BF)
            score = jnp.where(causal, dot(g0, v, 1, 1) / SPAN, 0.0).astype(BF)
            intra = dot(attend, v, 1, 0)
            zero = jnp.zeros((DK, DK), BF)
            level = jnp.where(upper, near_state[h], zero)
            back = jnp.where(upper, zero, near_grad[h])
            near = dot(q, level, 1, 0)
            part[0, :, lanes] = (w0 * intra + w1 * near).astype(BF)
            part[1, :, lanes] = (dot(score, k, 1, 0) + dot(g1, level, 1, 1)).astype(BF)
            part[2, :, lanes] = (dot(score, q, 0, 0) + dot(v, back, 1, 1)).astype(BF)
            part[3, :, lanes] = (dot(attend, g0, 0, 0) + dot(k, back, 1, 0)).astype(BF)
            total = jnp.where(to == h * 8, jnp.sum(gf * intra, -1, keepdims=True), total)
            total = jnp.where(to == h * 8 + 1, jnp.sum(gf * near, -1, keepdims=True), total)
        sums[s] = total


def along_z_body(meta, got, send):
    y = meta[2]
    totals = []
    for i in range(3, SLOTS):
        total = got[0, i].astype(F32)
        for z in range(1, 8):
            total = total + got[z, i].astype(F32)
        totals.append(total.astype(BF))
    send[y] = jnp.zeros_like(totals[0])
    for step in range(1, 8):
        send[y ^ step] = totals[step.bit_length() - 1]


def buckets_body(meta, got, from_y, down):
    y = meta[2]
    for i in range(3):
        width = 1 << i
        scale = 1.0 / (2 * width * SPAN)
        for block in range(8 // width):
            total = got[block * width, i].astype(F32)
            for z in range(block * width + 1, (block + 1) * width):
                total = total + got[z, i].astype(F32)
            total = (total * scale).astype(BF)
            target = block ^ 1
            for z in range(target * width, (target + 1) * width):
                down[z, i] = total
    for i in range(3):
        width = 1 << i
        scale = 1.0 / (16 * width * SPAN)
        total = from_y[y ^ width].astype(F32)
        for step in range(width + 1, 2 * width):
            total = total + from_y[y ^ step].astype(F32)
        total = (total * scale).astype(BF)
        for z in range(8):
            down[z, 3 + i] = total


def level_bits(meta):
    return [(meta[1 + i // 3] >> (i % 3)) & 1 for i in range(SLOTS)]


def bucket_sum(got, h, i):
    return jnp.concatenate([got[2 * h, i], got[2 * h + 1, i]], 0)


def outputs_body(
    meta, own, other, cols, chosen, part_own, part_other, sums, got, new_own, new_other, logit_grad, rows
):
    core = meta[0]
    bits = level_bits(meta)
    lane = lax.broadcasted_iota(jnp.int32, (2 * SPAN, 128), 1)
    both = jnp.concatenate([cols[0], cols[1]], 0)
    total = jnp.concatenate([sums[0], sums[1]], 0)
    for h in range(HALF):
        lanes = slice(h * DK, (h + 1) * DK)
        q = jnp.concatenate([own[0, :, lanes], other[0, :, lanes]], 0)
        gf = jnp.concatenate([own[3, :, lanes], other[3, :, lanes]], 0).astype(F32)
        levels = []
        for i in range(SLOTS):
            state = bucket_sum(got, h, i)
            levels.append(jnp.where(bits[i] == 1, state, jnp.zeros_like(state)))
        outs = dot(q, jnp.concatenate(levels, 1), 1, 0)
        mix = jnp.concatenate([part_own[0, :, lanes], part_other[0, :, lanes]], 0).astype(F32)
        for i in range(SLOTS):
            out = outs[:, i * DK : (i + 1) * DK]
            mix = mix + both[:, h * 8 + 2 + i : h * 8 + 3 + i] * out
            total = jnp.where(lane == h * 8 + 2 + i, jnp.sum(gf * out, -1, keepdims=True), total)
        new_own[0, :, lanes] = mix[:SPAN].astype(BF)
        new_other[0, :, lanes] = mix[SPAN:].astype(BF)
    for s in range(2):
        c = core if s == 0 else 1 - core
        by_level = jnp.transpose(total[s * SPAN : (s + 1) * SPAN])[: 8 * HALF]
        by_level = by_level * jax.nn.sigmoid(chosen[:, s * SPAN : (s + 1) * SPAN])
        for h in range(HALF):
            for l in range(8):
                rows[pl.ds(h * 8 + meta[3 + l], 1), :] = by_level[h * 8 + l : h * 8 + l + 1, :]
        ready = rows[...].astype(BF)
        for x in range(4):
            logit_grad[c * 4 + x] = ready


def grads_body(meta, own, other, cols, part_own, part_other, got, keep, send):
    bits = level_bits(meta)
    both = jnp.concatenate([cols[0], cols[1]], 0)
    for h in range(HALF):
        lanes = slice(h * DK, (h + 1) * DK)
        k, v, g = (
            jnp.concatenate([own[i, :, lanes], other[i, :, lanes]], 0) for i in range(1, 4)
        )
        gf = g.astype(F32)
        levels, weighted = [], []
        back = jnp.zeros((DK, DK), F32)
        for i in range(SLOTS):
            state = bucket_sum(got, h, i)
            zero = jnp.zeros_like(state)
            levels.append(jnp.where(bits[i] == 1, state, zero))
            back = back + jnp.where(bits[i] == 1, zero, state).astype(F32)
            weighted.append((both[:, h * 8 + 2 + i : h * 8 + 3 + i] * gf).astype(BF))
        back = back.astype(BF)
        found = (
            dot(jnp.concatenate(weighted, 1), jnp.concatenate(levels, 1), 1, 1),
            dot(v, back, 1, 1),
            dot(k, back, 1, 0),
        )
        for s, (part, dst) in enumerate(((part_own, keep), (part_other, send))):
            span = slice(s * SPAN, (s + 1) * SPAN)
            for i in range(3):
                dst[1 + i, :, lanes] = (
                    part[1 + i, :, lanes].astype(F32) + found[i][span]
                ).astype(BF)


def unpack_body(meta, keep, got, logit_grad, gate, mixed, dq, dk, dv, dhidden):
    first = meta[0] == 0
    for i, dst in enumerate((mixed, dq, dk, dv)):
        here, there = keep[i], got[i]
        dst[:, :LANES] = jnp.where(first, here, there)
        dst[:, LANES:] = jnp.where(first, there, here)
    grads = jnp.concatenate([logit_grad[c * 4 + x] for x in range(4) for c in range(2)], 0)
    dhidden[...] = dot(grads, gate[...], 0, 1).astype(BF)


def local(queries, keys, values, hidden, gate_weight, level_slot, out_grad):
    core, z, y = lax.axis_index("core"), lax.axis_index("z"), lax.axis_index("y")
    place = jnp.stack([core, z, y]).astype(jnp.int32)
    meta = jnp.concatenate([place, level_slot])
    swap = [(0, 1), (1, 0)]

    def exchange(array, axis):
        return lax.all_to_all(array, axis, 0, 0, tiled=True)

    send, own, partial = pl.pallas_call(
        pack_body,
        out_shape=(shape(4, SPAN, LANES), shape(4, SPAN, LANES), shape(8, 32, SPAN, kind=F32)),
        in_specs=smem(1) + hbm(6),
        out_specs=tuple(vmem(3)),
        scratch_shapes=[
            pltpu.VMEM((4, SPAN, 2 * LANES), BF),
            pltpu.VMEM(hidden.shape, BF),
            pltpu.VMEM(gate_weight.shape, BF),
            pltpu.SemaphoreType.DMA((11,)),
        ],
        compiler_params=SMALL,
        name="pack",
    )(meta, *far(queries, keys, values, out_grad, hidden, gate_weight))
    other = lax.ppermute(send, "core", swap)
    parts = exchange(partial, ("core", "head"))
    up, cols, chosen, near_state, near_grad = pl.pallas_call(
        states_body,
        out_shape=(
            shape(8, SLOTS, 64, DK),
            shape(2, SPAN, 128, kind=F32),
            shape(8 * HALF, 2 * SPAN, kind=F32),
            shape(HALF, DK, DK),
            shape(HALF, DK, DK),
        ),
        in_specs=smem(1) + vmem(3),
        out_specs=tuple(vmem(5)),
        scratch_shapes=[pltpu.VMEM((8 * HALF, 2 * SPAN), F32)],
        compiler_params=SMALL,
        name="states",
    )(meta, *near(parts, own, other))
    got = exchange(up, "z")
    part_own, part_other, sums = pl.pallas_call(
        local_body,
        out_shape=(shape(4, SPAN, LANES), shape(4, SPAN, LANES), shape(2, SPAN, 128, kind=F32)),
        in_specs=smem(1) + vmem(5),
        out_specs=tuple(vmem(3)),
        compiler_params=SMALL,
        name="local",
    )(meta, *near(own, other, cols, near_state, near_grad))
    to_y = pl.pallas_call(
        along_z_body,
        out_shape=shape(8, 64, DK),
        in_specs=smem(1) + vmem(1),
        out_specs=vmem(1)[0],
        compiler_params=SMALL,
        name="along_z",
    )(meta, *near(got))
    from_y = exchange(to_y, "y")
    down = pl.pallas_call(
        buckets_body,
        out_shape=shape(8, SLOTS, 64, DK),
        in_specs=smem(1) + vmem(2),
        out_specs=vmem(1)[0],
        compiler_params=SMALL,
        name="buckets",
    )(meta, *near(got, from_y))
    sums_here = exchange(down, "z")
    part_own, part_other, logit_grad = pl.pallas_call(
        outputs_body,
        out_shape=(shape(4, SPAN, LANES), shape(4, SPAN, LANES), shape(8, 8 * HALF, SPAN)),
        in_specs=smem(1) + vmem(8),
        out_specs=tuple(vmem(3)),
        scratch_shapes=[pltpu.VMEM((8 * HALF, SPAN), F32)],
        input_output_aliases={5: 0, 6: 1},
        compiler_params=SMALL,
        name="outputs",
    )(meta, *near(own, other, cols, chosen, part_own, part_other, sums, sums_here))
    all_grads = exchange(logit_grad, ("core", "head"))
    keep, away = pl.pallas_call(
        grads_body,
        out_shape=(shape(4, SPAN, LANES), shape(4, SPAN, LANES)),
        in_specs=smem(1) + vmem(6),
        out_specs=tuple(vmem(2)),
        input_output_aliases={4: 0, 5: 1},
        compiler_params=SMALL,
        name="grads",
    )(meta, *near(own, other, cols, part_own, part_other, sums_here))
    back = lax.ppermute(away, "core", swap)
    outs = (jax.ShapeDtypeStruct((SPAN, 2 * LANES), BF),) * 4
    return pl.pallas_call(
        unpack_body,
        out_shape=outs + (jax.ShapeDtypeStruct((SPAN, hidden.shape[1]), BF),),
        in_specs=smem(1) + vmem(4),
        out_specs=tuple(vmem(5)),
        compiler_params=SMALL,
        name="unpack",
    )(meta, *near(keep, back, all_grads), gate_weight)


def solution(mesh):
    names = ("y", "z", "core", "head")
    fine = Mesh(mesh.devices.reshape(8, 8, 2, 4), names)
    tokens = ("y", "z", "core")
    rows = P(tokens, "head")
    return jax.shard_map(
        local,
        mesh=fine,
        in_specs=(rows, rows, rows, rows, P("head", None), P(), rows),
        out_specs=(rows,) * 5,
        check_vma=False,
    )
```

```python
import jax
import jax.numpy as jnp
from jax import lax
from jax.experimental import pallas as pl
from jax.experimental.pallas import tpu as pltpu
from jax.sharding import Mesh, PartitionSpec as P


DK = 128
SPAN = 128
HALF = 4
LANES = HALF * DK
SLOTS = 6
DIRECT = 2
SPREAD = SLOTS - DIRECT
BF = jnp.bfloat16
F32 = jnp.float32


def dot(a, b, ca, cb):
    return lax.dot_general(a, b, (((ca,), (cb,)), ((), ())), preferred_element_type=F32)


def vmem(n):
    return [pl.BlockSpec(memory_space=pltpu.VMEM)] * n


def hbm(n):
    return [pl.BlockSpec(memory_space=pltpu.HBM)] * n


def smem(n):
    return [pl.BlockSpec(memory_space=pltpu.SMEM)] * n


def shape(*dims, kind=BF):
    return pltpu.VMEM(dims, kind)


def near(*arrays):
    return [pltpu.with_memory_space_constraint(a, pltpu.VMEM) for a in arrays]


def far(*arrays):
    return [pltpu.with_memory_space_constraint(a, pltpu.HBM) for a in arrays]


SMALL = pltpu.CompilerParams(vmem_limit_bytes=16 << 20)


def pack_body(q, k, v, g, hidden, gate, send, own, partial, held, held_hidden, held_gate, sems):
    copies = [
        pltpu.make_async_copy(hidden, held_hidden, sems.at[0]),
        pltpu.make_async_copy(gate.at[:256], held_gate.at[:256], sems.at[1]),
        pltpu.make_async_copy(gate.at[256:], held_gate.at[256:], sems.at[2]),
    ]
    for i, src in enumerate((q, k, v, g)):
        for part in range(2):
            rows = slice(part * 64, part * 64 + 64)
            copies.append(
                pltpu.make_async_copy(src.at[rows], held.at[i, rows], sems.at[3 + 2 * i + part])
            )
    for copy in copies:
        copy.start()
    for copy in copies[:3]:
        copy.wait()
    logits = dot(held_gate[...], held_hidden[...], 0, 1)
    for c in range(2):
        for x in range(4):
            row = x * 64 + c * 32
            partial[c * 4 + x] = logits[row : row + 32]
    first = lax.axis_index("core") == 0
    for i in range(4):
        copies[3 + 2 * i].wait()
        copies[4 + 2 * i].wait()
        low, high = held[i, :, :LANES], held[i, :, LANES:]
        own[i] = jnp.where(first, low, high)
        send[i] = jnp.where(first, high, low)


def states_body(meta, parts, own, other, up, pair, cols, chosen, near_state, near_grad, rows):
    core, z, y = meta[0], meta[1], meta[2]
    for s in range(2):
        c = core if s == 0 else 1 - core
        logits = parts[c * 4] + parts[c * 4 + 1] + parts[c * 4 + 2] + parts[c * 4 + 3]
        rows[:, s * SPAN : (s + 1) * SPAN] = logits
    for h in range(HALF):
        for l in range(8):
            chosen[h * 8 + l : h * 8 + l + 1, :] = rows[pl.ds(h * 8 + meta[3 + l], 1), :]
    x = chosen[...]
    weights = jnp.maximum(x, 0.0) + jnp.log1p(jnp.exp(-jnp.abs(x)))
    padded = jnp.concatenate([weights, jnp.zeros((128 - 8 * HALF, 2 * SPAN), F32)], 0)
    for s in range(2):
        cols[s] = jnp.transpose(padded[:, s * SPAN : (s + 1) * SPAN])
    both = jnp.concatenate([cols[0], cols[1]], 0)
    first = core == 0
    for h in range(HALF):
        lanes = slice(h * DK, (h + 1) * DK)
        q = jnp.concatenate([own[0, :, lanes], other[0, :, lanes]], 0)
        g = jnp.concatenate([own[3, :, lanes], other[3, :, lanes]], 0).astype(F32)
        state_own = dot(own[1, :, lanes], own[2, :, lanes], 0, 0)
        state_other = dot(other[1, :, lanes], other[2, :, lanes], 0, 0)
        state = state_own + state_other
        near_state[h] = (jnp.where(first, state_own, state_other) / SPAN).astype(BF)
        near = both[:, h * 8 + 1 : h * 8 + 2]
        near_g = (near * g).astype(BF)
        grad_own = dot(q[:SPAN], near_g[:SPAN], 0, 0)
        grad_other = dot(q[SPAN:], near_g[SPAN:], 0, 0)
        near_grad[h] = (jnp.where(first, grad_other, grad_own) / SPAN).astype(BF)
        weighted = jnp.concatenate(
            [(both[:, h * 8 + 2 + i : h * 8 + 3 + i] * g).astype(BF) for i in range(SLOTS)], 1
        )
        grads = dot(q, weighted, 0, 0)
        for i in range(SLOTS):
            bit = (z >> i) & 1 if i < 3 else (y >> (i - 3)) & 1
            piece = jnp.where(bit == 1, grads[:, i * DK : (i + 1) * DK], state).astype(BF)
            if i < DIRECT:
                pair[i, h] = piece
            else:
                up[2 * h, i - DIRECT] = piece[:64]
                up[2 * h + 1, i - DIRECT] = piece[64:]


def local_body(meta, own, other, cols, near_state, near_grad, part_own, part_other, sums):
    core = meta[0]
    at = lax.broadcasted_iota(jnp.int32, (SPAN, SPAN), 0)
    to = lax.broadcasted_iota(jnp.int32, (SPAN, SPAN), 1)
    causal = at >= to
    for s, (src, part) in enumerate(((own, part_own), (other, part_other))):
        upper = (core == 1) if s == 0 else (core == 0)
        total = jnp.zeros((SPAN, 128), F32)
        weights = cols[s]
        for h in range(HALF):
            lanes = slice(h * DK, (h + 1) * DK)
            q, k, v, g = (src[i, :, lanes] for i in range(4))
            gf = g.astype(F32)
            w0 = weights[:, h * 8 : h * 8 + 1]
            w1 = weights[:, h * 8 + 1 : h * 8 + 2]
            g0 = (w0 * gf).astype(BF)
            g1 = (w1 * gf).astype(BF)
            attend = jnp.where(causal, dot(q, k, 1, 1) / SPAN, 0.0).astype(BF)
            score = jnp.where(causal, dot(g0, v, 1, 1) / SPAN, 0.0).astype(BF)
            intra = dot(attend, v, 1, 0)
            zero = jnp.zeros((DK, DK), BF)
            level = jnp.where(upper, near_state[h], zero)
            back = jnp.where(upper, zero, near_grad[h])
            near = dot(q, level, 1, 0)
            part[0, :, lanes] = (w0 * intra + w1 * near).astype(BF)
            part[1, :, lanes] = (dot(score, k, 1, 0) + dot(g1, level, 1, 1)).astype(BF)
            part[2, :, lanes] = (dot(score, q, 0, 0) + dot(v, back, 1, 1)).astype(BF)
            part[3, :, lanes] = (dot(attend, g0, 0, 0) + dot(k, back, 1, 0)).astype(BF)
            total = jnp.where(to == h * 8, jnp.sum(gf * intra, -1, keepdims=True), total)
            total = jnp.where(to == h * 8 + 1, jnp.sum(gf * near, -1, keepdims=True), total)
        sums[s] = total


def along_z_body(meta, got, send, halves):
    y = meta[2]
    totals = []
    for i in range(SPREAD - 3, SPREAD):
        total = got[0, i].astype(F32)
        for z in range(1, 8):
            total = total + got[z, i].astype(F32)
        totals.append(total.astype(BF))
    send[y] = jnp.zeros_like(totals[0])
    for step in range(1, 8):
        send[y ^ step] = totals[step.bit_length() - 1]
    for half in range(2):
        total = got[4 * half, 0].astype(F32)
        for z in range(4 * half + 1, 4 * half + 4):
            total = total + got[z, 0].astype(F32)
        halves[half] = (total * (1.0 / (8 * SPAN))).astype(BF)


def pair_body(pair, pair_got, pair_sum):
    for h in range(HALF):
        pair_sum[h] = (pair[1, h].astype(F32) + pair_got[1, h].astype(F32)).astype(BF)


def buckets_body(meta, halves, from_y, pair_got, quad_got, down, direct):
    y = meta[2]
    for z in range(8):
        down[z, 0] = halves[1 - z // 4]
    for i in range(3):
        width = 1 << i
        total = from_y[y ^ width].astype(F32)
        for step in range(width + 1, 2 * width):
            total = total + from_y[y ^ step].astype(F32)
        total = (total * (1.0 / (16 * width * SPAN))).astype(BF)
        for z in range(8):
            down[z, 1 + i] = total
    for h in range(HALF):
        direct[0, h] = pair_got[0, h] * (1.0 / (2 * SPAN))
        direct[1, h] = quad_got[h] * (1.0 / (4 * SPAN))


def level_bits(meta):
    return [(meta[1 + i // 3] >> (i % 3)) & 1 for i in range(SLOTS)]


def bucket_sum(direct, got, h, i):
    if i < DIRECT:
        return direct[i, h]
    return jnp.concatenate([got[2 * h, i - DIRECT], got[2 * h + 1, i - DIRECT]], 0)


def outputs_body(
    meta, own, other, cols, chosen, part_own, part_other, sums, direct, got,
    new_own, new_other, logit_grad, rows,
):
    core = meta[0]
    bits = level_bits(meta)
    lane = lax.broadcasted_iota(jnp.int32, (2 * SPAN, 128), 1)
    both = jnp.concatenate([cols[0], cols[1]], 0)
    total = jnp.concatenate([sums[0], sums[1]], 0)
    for h in range(HALF):
        lanes = slice(h * DK, (h + 1) * DK)
        q = jnp.concatenate([own[0, :, lanes], other[0, :, lanes]], 0)
        gf = jnp.concatenate([own[3, :, lanes], other[3, :, lanes]], 0).astype(F32)
        levels = []
        for i in range(SLOTS):
            state = bucket_sum(direct, got, h, i)
            levels.append(jnp.where(bits[i] == 1, state, jnp.zeros_like(state)))
        outs = dot(q, jnp.concatenate(levels, 1), 1, 0)
        mix = jnp.concatenate([part_own[0, :, lanes], part_other[0, :, lanes]], 0).astype(F32)
        for i in range(SLOTS):
            out = outs[:, i * DK : (i + 1) * DK]
            mix = mix + both[:, h * 8 + 2 + i : h * 8 + 3 + i] * out
            total = jnp.where(lane == h * 8 + 2 + i, jnp.sum(gf * out, -1, keepdims=True), total)
        new_own[0, :, lanes] = mix[:SPAN].astype(BF)
        new_other[0, :, lanes] = mix[SPAN:].astype(BF)
    for s in range(2):
        c = core if s == 0 else 1 - core
        by_level = jnp.transpose(total[s * SPAN : (s + 1) * SPAN])[: 8 * HALF]
        by_level = by_level * jax.nn.sigmoid(chosen[:, s * SPAN : (s + 1) * SPAN])
        for h in range(HALF):
            for l in range(8):
                rows[pl.ds(h * 8 + meta[3 + l], 1), :] = by_level[h * 8 + l : h * 8 + l + 1, :]
        ready = rows[...].astype(BF)
        for x in range(4):
            logit_grad[c * 4 + x] = ready


def grads_body(meta, own, other, cols, part_own, part_other, direct, got, keep, send):
    bits = level_bits(meta)
    both = jnp.concatenate([cols[0], cols[1]], 0)
    for h in range(HALF):
        lanes = slice(h * DK, (h + 1) * DK)
        k, v, g = (
            jnp.concatenate([own[i, :, lanes], other[i, :, lanes]], 0) for i in range(1, 4)
        )
        gf = g.astype(F32)
        levels, weighted = [], []
        back = jnp.zeros((DK, DK), F32)
        for i in range(SLOTS):
            state = bucket_sum(direct, got, h, i)
            zero = jnp.zeros_like(state)
            levels.append(jnp.where(bits[i] == 1, state, zero))
            back = back + jnp.where(bits[i] == 1, zero, state).astype(F32)
            weighted.append((both[:, h * 8 + 2 + i : h * 8 + 3 + i] * gf).astype(BF))
        back = back.astype(BF)
        found = (
            dot(jnp.concatenate(weighted, 1), jnp.concatenate(levels, 1), 1, 1),
            dot(v, back, 1, 1),
            dot(k, back, 1, 0),
        )
        for s, (part, dst) in enumerate(((part_own, keep), (part_other, send))):
            span = slice(s * SPAN, (s + 1) * SPAN)
            for i in range(3):
                dst[1 + i, :, lanes] = (
                    part[1 + i, :, lanes].astype(F32) + found[i][span]
                ).astype(BF)


def unpack_body(meta, keep, got, logit_grad, gate, mixed, dq, dk, dv, dhidden):
    first = meta[0] == 0
    for i, dst in enumerate((mixed, dq, dk, dv)):
        here, there = keep[i], got[i]
        dst[:, :LANES] = jnp.where(first, here, there)
        dst[:, LANES:] = jnp.where(first, there, here)
    grads = jnp.concatenate([logit_grad[c * 4 + x] for x in range(4) for c in range(2)], 0)
    dhidden[...] = dot(grads, gate[...], 0, 1).astype(BF)


def local(queries, keys, values, hidden, gate_weight, level_slot, out_grad):
    core, z, y = lax.axis_index("core"), lax.axis_index("z"), lax.axis_index("y")
    place = jnp.stack([core, z, y]).astype(jnp.int32)
    meta = jnp.concatenate([place, level_slot])
    swap = [(0, 1), (1, 0)]

    def exchange(array, axis):
        return lax.all_to_all(array, axis, 0, 0, tiled=True)

    def flip(array, distance):
        return lax.ppermute(array, "z", [(i, i ^ distance) for i in range(8)])

    send, own, partial = pl.pallas_call(
        pack_body,
        out_shape=(shape(4, SPAN, LANES), shape(4, SPAN, LANES), shape(8, 32, SPAN, kind=F32)),
        in_specs=hbm(6),
        out_specs=tuple(vmem(3)),
        scratch_shapes=[
            pltpu.VMEM((4, SPAN, 2 * LANES), BF),
            pltpu.VMEM(hidden.shape, BF),
            pltpu.VMEM(gate_weight.shape, BF),
            pltpu.SemaphoreType.DMA((11,)),
        ],
        compiler_params=SMALL,
        name="pack",
    )(*far(queries, keys, values, out_grad, hidden, gate_weight))
    other = lax.ppermute(send, "core", swap)
    parts = exchange(partial, ("core", "head"))
    up, pair, cols, chosen, near_state, near_grad = pl.pallas_call(
        states_body,
        out_shape=(
            shape(8, SPREAD, 64, DK),
            shape(DIRECT, HALF, DK, DK),
            shape(2, SPAN, 128, kind=F32),
            shape(8 * HALF, 2 * SPAN, kind=F32),
            shape(HALF, DK, DK),
            shape(HALF, DK, DK),
        ),
        in_specs=smem(1) + vmem(3),
        out_specs=tuple(vmem(6)),
        scratch_shapes=[pltpu.VMEM((8 * HALF, 2 * SPAN), F32)],
        compiler_params=SMALL,
        name="states",
    )(meta, *near(parts, own, other))
    pair_got = flip(pair, 1)
    got = exchange(up, "z")
    to_y, halves = pl.pallas_call(
        along_z_body,
        out_shape=(shape(8, 64, DK), shape(2, 64, DK)),
        in_specs=smem(1) + vmem(1),
        out_specs=tuple(vmem(2)),
        compiler_params=SMALL,
        name="along_z",
    )(meta, *near(got))
    pair_sum = pl.pallas_call(
        pair_body,
        out_shape=shape(HALF, DK, DK),
        in_specs=vmem(2),
        out_specs=vmem(1)[0],
        compiler_params=SMALL,
        name="pair",
    )(*near(pair, pair_got))
    quad_got = flip(pair_sum, 2)
    from_y = exchange(to_y, "y")
    part_own, part_other, sums = pl.pallas_call(
        local_body,
        out_shape=(shape(4, SPAN, LANES), shape(4, SPAN, LANES), shape(2, SPAN, 128, kind=F32)),
        in_specs=smem(1) + vmem(5),
        out_specs=tuple(vmem(3)),
        compiler_params=SMALL,
        name="local",
    )(meta, *near(own, other, cols, near_state, near_grad))
    down, direct = pl.pallas_call(
        buckets_body,
        out_shape=(shape(8, SPREAD, 64, DK), shape(DIRECT, HALF, DK, DK)),
        in_specs=smem(1) + vmem(4),
        out_specs=tuple(vmem(2)),
        compiler_params=SMALL,
        name="buckets",
    )(meta, *near(halves, from_y, pair_got, quad_got))
    sums_here = exchange(down, "z")
    part_own, part_other, logit_grad = pl.pallas_call(
        outputs_body,
        out_shape=(shape(4, SPAN, LANES), shape(4, SPAN, LANES), shape(8, 8 * HALF, SPAN)),
        in_specs=smem(1) + vmem(9),
        out_specs=tuple(vmem(3)),
        scratch_shapes=[pltpu.VMEM((8 * HALF, SPAN), F32)],
        input_output_aliases={5: 0, 6: 1},
        compiler_params=SMALL,
        name="outputs",
    )(meta, *near(own, other, cols, chosen, part_own, part_other, sums, direct, sums_here))
    all_grads = exchange(logit_grad, ("core", "head"))
    keep, away = pl.pallas_call(
        grads_body,
        out_shape=(shape(4, SPAN, LANES), shape(4, SPAN, LANES)),
        in_specs=smem(1) + vmem(7),
        out_specs=tuple(vmem(2)),
        input_output_aliases={4: 0, 5: 1},
        compiler_params=SMALL,
        name="grads",
    )(meta, *near(own, other, cols, part_own, part_other, direct, sums_here))
    back = lax.ppermute(away, "core", swap)
    outs = (jax.ShapeDtypeStruct((SPAN, 2 * LANES), BF),) * 4
    return pl.pallas_call(
        unpack_body,
        out_shape=outs + (jax.ShapeDtypeStruct((SPAN, hidden.shape[1]), BF),),
        in_specs=smem(1) + vmem(4),
        out_specs=tuple(vmem(5)),
        compiler_params=SMALL,
        name="unpack",
    )(meta, *near(keep, back, all_grads), gate_weight)


def solution(mesh):
    names = ("y", "z", "core", "head")
    fine = Mesh(mesh.devices.reshape(8, 8, 2, 4), names)
    tokens = ("y", "z", "core")
    rows = P(tokens, "head")
    return jax.shard_map(
        local,
        mesh=fine,
        in_specs=(rows, rows, rows, rows, P("head", None), P(), rows),
        out_specs=(rows,) * 5,
        check_vma=False,
    )
```

```python
import jax
import jax.numpy as jnp
from jax import lax
from jax.experimental import pallas as pl
from jax.experimental.pallas import tpu as pltpu
from jax.sharding import Mesh, PartitionSpec as P


DK = 128
SPAN = 128
HALF = 4
LANES = HALF * DK
SLOTS = 6
DIRECT = 2
SPREAD = SLOTS - DIRECT
BF = jnp.bfloat16
F32 = jnp.float32


def dot(a, b, ca, cb):
    return lax.dot_general(a, b, (((ca,), (cb,)), ((), ())), preferred_element_type=F32)


def vmem(n):
    return [pl.BlockSpec(memory_space=pltpu.VMEM)] * n


def hbm(n):
    return [pl.BlockSpec(memory_space=pltpu.HBM)] * n


def smem(n):
    return [pl.BlockSpec(memory_space=pltpu.SMEM)] * n


def shape(*dims, kind=BF):
    return pltpu.VMEM(dims, kind)


def near(*arrays):
    return [pltpu.with_memory_space_constraint(a, pltpu.VMEM) for a in arrays]


def far(*arrays):
    return [pltpu.with_memory_space_constraint(a, pltpu.HBM) for a in arrays]


SMALL = pltpu.CompilerParams(vmem_limit_bytes=16 << 20)


def pack_body(q, k, v, g, hidden, gate, send, own, partial, held, held_hidden, held_gate, sems):
    copies = [
        pltpu.make_async_copy(hidden, held_hidden, sems.at[0]),
        pltpu.make_async_copy(gate.at[:256], held_gate.at[:256], sems.at[1]),
        pltpu.make_async_copy(gate.at[256:], held_gate.at[256:], sems.at[2]),
    ]
    for i, src in enumerate((q, k, v, g)):
        for part in range(2):
            rows = slice(part * 64, part * 64 + 64)
            copies.append(
                pltpu.make_async_copy(src.at[rows], held.at[i, rows], sems.at[3 + 2 * i + part])
            )
    for copy in copies:
        copy.start()
    for copy in copies[:3]:
        copy.wait()
    logits = dot(held_gate[...], held_hidden[...], 0, 1)
    for c in range(2):
        for x in range(4):
            row = x * 64 + c * 32
            partial[c * 4 + x] = logits[row : row + 32]
    first = lax.axis_index("core") == 0
    for i in range(4):
        copies[3 + 2 * i].wait()
        copies[4 + 2 * i].wait()
        low, high = held[i, :, :LANES], held[i, :, LANES:]
        own[i] = jnp.where(first, low, high)
        send[i] = jnp.where(first, high, low)


def pre_body(own, other, state, near_state):
    first = lax.axis_index("core") == 0
    for h in range(HALF):
        lanes = slice(h * DK, (h + 1) * DK)
        state_own = dot(own[1, :, lanes], own[2, :, lanes], 0, 0)
        state_other = dot(other[1, :, lanes], other[2, :, lanes], 0, 0)
        state[h] = (state_own + state_other).astype(BF)
        near_state[h] = (jnp.where(first, state_own, state_other) / SPAN).astype(BF)


def states_body(meta, parts, own, other, state, up, pair, cols, logits, near_grad, chosen):
    core, z, y = meta[0], meta[1], meta[2]
    for s in range(2):
        c = core if s == 0 else 1 - core
        total = parts[c * 4] + parts[c * 4 + 1] + parts[c * 4 + 2] + parts[c * 4 + 3]
        logits[:, s * SPAN : (s + 1) * SPAN] = total
    for h in range(HALF):
        for l in range(8):
            chosen[h * 8 + l : h * 8 + l + 1, :] = logits[pl.ds(h * 8 + meta[3 + l], 1), :]
    x = chosen[...]
    weights = jnp.maximum(x, 0.0) + jnp.log1p(jnp.exp(-jnp.abs(x)))
    padded = jnp.concatenate([weights, jnp.zeros((128 - 8 * HALF, 2 * SPAN), F32)], 0)
    for s in range(2):
        cols[s] = jnp.transpose(padded[:, s * SPAN : (s + 1) * SPAN])
    both = jnp.concatenate([cols[0], cols[1]], 0)
    first = core == 0
    for h in range(HALF):
        lanes = slice(h * DK, (h + 1) * DK)
        q = jnp.concatenate([own[0, :, lanes], other[0, :, lanes]], 0)
        g = jnp.concatenate([own[3, :, lanes], other[3, :, lanes]], 0).astype(F32)
        near = both[:, h * 8 + 1 : h * 8 + 2]
        near_g = (near * g).astype(BF)
        grad_own = dot(q[:SPAN], near_g[:SPAN], 0, 0)
        grad_other = dot(q[SPAN:], near_g[SPAN:], 0, 0)
        near_grad[h] = (jnp.where(first, grad_other, grad_own) / SPAN).astype(BF)
        weighted = jnp.concatenate(
            [(both[:, h * 8 + 2 + i : h * 8 + 3 + i] * g).astype(BF) for i in range(SLOTS)], 1
        )
        grads = dot(q, weighted, 0, 0)
        held = state[h]
        for i in range(SLOTS):
            bit = (z >> i) & 1 if i < 3 else (y >> (i - 3)) & 1
            piece = jnp.where(bit == 1, grads[:, i * DK : (i + 1) * DK].astype(BF), held)
            if i < DIRECT:
                pair[i, h] = piece
            else:
                up[2 * h, i - DIRECT] = piece[:64]
                up[2 * h + 1, i - DIRECT] = piece[64:]


def row_picker(meta, h, levels):
    row = lax.broadcasted_iota(jnp.int32, (8 * HALF, DK), 0)
    return jnp.concatenate(
        [jnp.where(row == h * 8 + meta[3 + l], 1.0, 0.0).astype(BF) for l in levels], 1
    )


def local_body(meta, own, other, cols, near_state, near_grad, part_own, part_other, sums):
    core = meta[0]
    at = lax.broadcasted_iota(jnp.int32, (SPAN, SPAN), 0)
    causal = at >= lax.broadcasted_iota(jnp.int32, (SPAN, SPAN), 1)
    for s, (src, part) in enumerate(((own, part_own), (other, part_other))):
        upper = (core == 1) if s == 0 else (core == 0)
        total = jnp.zeros((8 * HALF, SPAN), F32)
        weights = cols[s]
        for h in range(HALF):
            lanes = slice(h * DK, (h + 1) * DK)
            q, k, v, g = (src[i, :, lanes] for i in range(4))
            gf = g.astype(F32)
            w0 = weights[:, h * 8 : h * 8 + 1]
            w1 = weights[:, h * 8 + 1 : h * 8 + 2]
            g0 = (w0 * gf).astype(BF)
            g1 = (w1 * gf).astype(BF)
            attend = jnp.where(causal, dot(q, k, 1, 1) / SPAN, 0.0).astype(BF)
            score = jnp.where(causal, dot(g0, v, 1, 1) / SPAN, 0.0).astype(BF)
            intra = dot(attend, v, 1, 0)
            zero = jnp.zeros((DK, DK), BF)
            level = jnp.where(upper, near_state[h], zero)
            back = jnp.where(upper, zero, near_grad[h])
            near = dot(q, level, 1, 0)
            part[0, :, lanes] = (w0 * intra + w1 * near).astype(BF)
            part[1, :, lanes] = (dot(score, k, 1, 0) + dot(g1, level, 1, 1)).astype(BF)
            part[2, :, lanes] = (dot(score, q, 0, 0) + dot(v, back, 1, 1)).astype(BF)
            part[3, :, lanes] = (dot(attend, g0, 0, 0) + dot(k, back, 1, 0)).astype(BF)
            products = jnp.concatenate([(gf * intra).astype(BF), (gf * near).astype(BF)], 1)
            total = total + dot(row_picker(meta, h, (0, 1)), products, 1, 1)
        sums[:, s * SPAN : (s + 1) * SPAN] = total


def along_z_body(meta, got, send, halves):
    y = meta[2]
    totals = []
    for i in range(SPREAD - 3, SPREAD):
        total = got[0, i].astype(F32)
        for z in range(1, 8):
            total = total + got[z, i].astype(F32)
        totals.append(total.astype(BF))
    send[y] = jnp.zeros_like(totals[0])
    for step in range(1, 8):
        send[y ^ step] = totals[step.bit_length() - 1]
    for half in range(2):
        total = got[4 * half, 0].astype(F32)
        for z in range(4 * half + 1, 4 * half + 4):
            total = total + got[z, 0].astype(F32)
        halves[half] = (total * (1.0 / (8 * SPAN))).astype(BF)


def pair_body(pair, pair_got, pair_sum):
    for h in range(HALF):
        pair_sum[h] = (pair[1, h].astype(F32) + pair_got[1, h].astype(F32)).astype(BF)


def buckets_body(meta, halves, from_y, pair_got, quad_got, down, direct):
    y = meta[2]
    for z in range(8):
        down[z, 0] = halves[1 - z // 4]
    for i in range(3):
        width = 1 << i
        total = from_y[y ^ width].astype(F32)
        for step in range(width + 1, 2 * width):
            total = total + from_y[y ^ step].astype(F32)
        total = (total * (1.0 / (16 * width * SPAN))).astype(BF)
        for z in range(8):
            down[z, 1 + i] = total
    for h in range(HALF):
        direct[0, h] = pair_got[0, h] * (1.0 / (2 * SPAN))
        direct[1, h] = quad_got[h] * (1.0 / (4 * SPAN))


def level_bits(meta):
    return [(meta[1 + i // 3] >> (i % 3)) & 1 for i in range(SLOTS)]


def bucket_sum(direct, got, h, i):
    if i < DIRECT:
        return direct[i, h]
    return jnp.concatenate([got[2 * h, i - DIRECT], got[2 * h + 1, i - DIRECT]], 0)


def outputs_body(
    meta, own, other, cols, logits, part_own, part_other, sums, direct, got,
    new_own, new_other, logit_grad,
):
    core = meta[0]
    bits = level_bits(meta)
    both = jnp.concatenate([cols[0], cols[1]], 0)
    total = sums[...]
    for h in range(HALF):
        lanes = slice(h * DK, (h + 1) * DK)
        q = jnp.concatenate([own[0, :, lanes], other[0, :, lanes]], 0)
        gf = jnp.concatenate([own[3, :, lanes], other[3, :, lanes]], 0).astype(F32)
        levels = []
        for i in range(SLOTS):
            state = bucket_sum(direct, got, h, i)
            levels.append(jnp.where(bits[i] == 1, state, jnp.zeros_like(state)))
        outs = dot(q, jnp.concatenate(levels, 1), 1, 0)
        mix = jnp.concatenate([part_own[0, :, lanes], part_other[0, :, lanes]], 0).astype(F32)
        products = []
        for i in range(SLOTS):
            out = outs[:, i * DK : (i + 1) * DK]
            mix = mix + both[:, h * 8 + 2 + i : h * 8 + 3 + i] * out
            products.append((gf * out).astype(BF))
        total = total + dot(
            row_picker(meta, h, range(2, 8)), jnp.concatenate(products, 1), 1, 1
        )
        new_own[0, :, lanes] = mix[:SPAN].astype(BF)
        new_other[0, :, lanes] = mix[SPAN:].astype(BF)
    ready = (total * jax.nn.sigmoid(logits[...])).astype(BF)
    for s in range(2):
        c = core if s == 0 else 1 - core
        for x in range(4):
            logit_grad[c * 4 + x] = ready[:, s * SPAN : (s + 1) * SPAN]


def grads_body(meta, own, other, cols, part_own, part_other, direct, got, keep, send):
    bits = level_bits(meta)
    both = jnp.concatenate([cols[0], cols[1]], 0)
    for h in range(HALF):
        lanes = slice(h * DK, (h + 1) * DK)
        k, v, g = (
            jnp.concatenate([own[i, :, lanes], other[i, :, lanes]], 0) for i in range(1, 4)
        )
        gf = g.astype(F32)
        levels, weighted = [], []
        back = jnp.zeros((DK, DK), F32)
        for i in range(SLOTS):
            state = bucket_sum(direct, got, h, i)
            zero = jnp.zeros_like(state)
            levels.append(jnp.where(bits[i] == 1, state, zero))
            back = back + jnp.where(bits[i] == 1, zero, state).astype(F32)
            weighted.append((both[:, h * 8 + 2 + i : h * 8 + 3 + i] * gf).astype(BF))
        back = back.astype(BF)
        found = (
            dot(jnp.concatenate(weighted, 1), jnp.concatenate(levels, 1), 1, 1),
            dot(v, back, 1, 1),
            dot(k, back, 1, 0),
        )
        for s, (part, dst) in enumerate(((part_own, keep), (part_other, send))):
            span = slice(s * SPAN, (s + 1) * SPAN)
            for i in range(3):
                dst[1 + i, :, lanes] = (
                    part[1 + i, :, lanes].astype(F32) + found[i][span]
                ).astype(BF)


def first_body(keep, logit_grad, gate, mixed, dq, dk, dv, dhidden, sems):
    mine = pl.multiple_of(lax.axis_index("core") * LANES, LANES)
    copies = [
        pltpu.make_async_copy(keep.at[i], dst.at[:, pl.ds(mine, LANES)], sems.at[i])
        for i, dst in enumerate((mixed, dq, dk, dv))
    ]
    for copy in copies:
        copy.start()
    grads = jnp.concatenate([logit_grad[c * 4 + x] for x in range(4) for c in range(2)], 0)
    dhidden[...] = dot(grads, gate[...], 0, 1).astype(BF)
    for copy in copies:
        copy.wait()


def second_body(got, old_mixed, old_dq, old_dk, old_dv, mixed, dq, dk, dv, sems):
    theirs = pl.multiple_of((1 - lax.axis_index("core")) * LANES, LANES)
    copies = [
        pltpu.make_async_copy(got.at[i], dst.at[:, pl.ds(theirs, LANES)], sems.at[i])
        for i, dst in enumerate((mixed, dq, dk, dv))
    ]
    for copy in copies:
        copy.start()
    for copy in copies:
        copy.wait()


def local(queries, keys, values, hidden, gate_weight, level_slot, out_grad):
    core, z, y = lax.axis_index("core"), lax.axis_index("z"), lax.axis_index("y")
    place = jnp.stack([core, z, y]).astype(jnp.int32)
    meta = jnp.concatenate([place, level_slot])
    swap = [(0, 1), (1, 0)]

    def exchange(array, axis):
        return lax.all_to_all(array, axis, 0, 0, tiled=True)

    def flip(array, distance):
        return lax.ppermute(array, "z", [(i, i ^ distance) for i in range(8)])

    send, own, partial = pl.pallas_call(
        pack_body,
        out_shape=(shape(4, SPAN, LANES), shape(4, SPAN, LANES), shape(8, 32, SPAN, kind=F32)),
        in_specs=hbm(6),
        out_specs=tuple(vmem(3)),
        scratch_shapes=[
            pltpu.VMEM((4, SPAN, 2 * LANES), BF),
            pltpu.VMEM(hidden.shape, BF),
            pltpu.VMEM(gate_weight.shape, BF),
            pltpu.SemaphoreType.DMA((11,)),
        ],
        compiler_params=SMALL,
        name="pack",
    )(*far(queries, keys, values, out_grad, hidden, gate_weight))
    other = lax.ppermute(send, "core", swap)
    parts = exchange(partial, ("core", "head"))
    state, near_state = pl.pallas_call(
        pre_body,
        out_shape=(shape(HALF, DK, DK), shape(HALF, DK, DK)),
        in_specs=vmem(2),
        out_specs=tuple(vmem(2)),
        compiler_params=SMALL,
        name="pre",
    )(*near(own, other))
    up, pair, cols, logits, near_grad = pl.pallas_call(
        states_body,
        out_shape=(
            shape(8, SPREAD, 64, DK),
            shape(DIRECT, HALF, DK, DK),
            shape(2, SPAN, 128, kind=F32),
            shape(8 * HALF, 2 * SPAN, kind=F32),
            shape(HALF, DK, DK),
        ),
        in_specs=smem(1) + vmem(4),
        out_specs=tuple(vmem(5)),
        scratch_shapes=[pltpu.VMEM((8 * HALF, 2 * SPAN), F32)],
        compiler_params=SMALL,
        name="states",
    )(meta, *near(parts, own, other, state))
    pair_got = flip(pair, 1)
    got = exchange(up, "z")
    to_y, halves = pl.pallas_call(
        along_z_body,
        out_shape=(shape(8, 64, DK), shape(2, 64, DK)),
        in_specs=smem(1) + vmem(1),
        out_specs=tuple(vmem(2)),
        compiler_params=SMALL,
        name="along_z",
    )(meta, *near(got))
    pair_sum = pl.pallas_call(
        pair_body,
        out_shape=shape(HALF, DK, DK),
        in_specs=vmem(2),
        out_specs=vmem(1)[0],
        compiler_params=SMALL,
        name="pair",
    )(*near(pair, pair_got))
    quad_got = flip(pair_sum, 2)
    from_y = exchange(to_y, "y")
    part_own, part_other, sums = pl.pallas_call(
        local_body,
        out_shape=(
            shape(4, SPAN, LANES),
            shape(4, SPAN, LANES),
            shape(8 * HALF, 2 * SPAN, kind=F32),
        ),
        in_specs=smem(1) + vmem(5),
        out_specs=tuple(vmem(3)),
        compiler_params=SMALL,
        name="local",
    )(meta, *near(own, other, cols, near_state, near_grad))
    down, direct = pl.pallas_call(
        buckets_body,
        out_shape=(shape(8, SPREAD, 64, DK), shape(DIRECT, HALF, DK, DK)),
        in_specs=smem(1) + vmem(4),
        out_specs=tuple(vmem(2)),
        compiler_params=SMALL,
        name="buckets",
    )(meta, *near(halves, from_y, pair_got, quad_got))
    sums_here = exchange(down, "z")
    part_own, part_other, logit_grad = pl.pallas_call(
        outputs_body,
        out_shape=(shape(4, SPAN, LANES), shape(4, SPAN, LANES), shape(8, 8 * HALF, SPAN)),
        in_specs=smem(1) + vmem(9),
        out_specs=tuple(vmem(3)),
        input_output_aliases={5: 0, 6: 1},
        compiler_params=SMALL,
        name="outputs",
    )(meta, *near(own, other, cols, logits, part_own, part_other, sums, direct, sums_here))
    all_grads = exchange(logit_grad, ("core", "head"))
    keep, away = pl.pallas_call(
        grads_body,
        out_shape=(shape(4, SPAN, LANES), shape(4, SPAN, LANES)),
        in_specs=smem(1) + vmem(7),
        out_specs=tuple(vmem(2)),
        input_output_aliases={4: 0, 5: 1},
        compiler_params=SMALL,
        name="grads",
    )(meta, *near(own, other, cols, part_own, part_other, direct, sums_here))
    back = lax.ppermute(away, "core", swap)
    wide = pltpu.HBM((SPAN, 2 * LANES), BF)
    *outs, dhidden = pl.pallas_call(
        first_body,
        out_shape=(wide,) * 4 + (jax.ShapeDtypeStruct((SPAN, hidden.shape[1]), BF),),
        in_specs=vmem(3),
        out_specs=tuple(hbm(4) + vmem(1)),
        scratch_shapes=[pltpu.SemaphoreType.DMA((4,))],
        compiler_params=SMALL,
        name="first",
    )(*near(keep, all_grads), gate_weight)
    outs = pl.pallas_call(
        second_body,
        out_shape=(wide,) * 4,
        in_specs=vmem(1) + hbm(4),
        out_specs=tuple(hbm(4)),
        input_output_aliases={1: 0, 2: 1, 3: 2, 4: 3},
        scratch_shapes=[pltpu.SemaphoreType.DMA((4,))],
        compiler_params=SMALL,
        name="second",
    )(*near(back), *far(*outs))
    return (*outs, dhidden)


def solution(mesh):
    names = ("y", "z", "core", "head")
    fine = Mesh(mesh.devices.reshape(8, 8, 2, 4), names)
    tokens = ("y", "z", "core")
    rows = P(tokens, "head")
    return jax.shard_map(
        local,
        mesh=fine,
        in_specs=(rows, rows, rows, rows, P("head", None), P(), rows),
        out_specs=(rows,) * 5,
        check_vma=False,
    )
```

```python
import jax
import jax.numpy as jnp
from jax import lax
from jax.experimental import pallas as pl
from jax.experimental.pallas import tpu as pltpu
from jax.sharding import Mesh, PartitionSpec as P


DK = 128
SPAN = 128
HALF = 4
LANES = HALF * DK
SLOTS = 6
DIRECT = 2
SPREAD = SLOTS - DIRECT
BF = jnp.bfloat16
F32 = jnp.float32


def dot(a, b, ca, cb):
    return lax.dot_general(a, b, (((ca,), (cb,)), ((), ())), preferred_element_type=F32)


def vmem(n):
    return [pl.BlockSpec(memory_space=pltpu.VMEM)] * n


def hbm(n):
    return [pl.BlockSpec(memory_space=pltpu.HBM)] * n


def smem(n):
    return [pl.BlockSpec(memory_space=pltpu.SMEM)] * n


def shape(*dims, kind=BF):
    return pltpu.VMEM(dims, kind)


def near(*arrays):
    return [pltpu.with_memory_space_constraint(a, pltpu.VMEM) for a in arrays]


def far(*arrays):
    return [pltpu.with_memory_space_constraint(a, pltpu.HBM) for a in arrays]


SMALL = pltpu.CompilerParams(vmem_limit_bytes=16 << 20)


def logits_body(hidden, gate, g, partial, held_g, held_hidden, held_gate, sems):
    copies = []
    for part in range(4):
        rows = slice(part * 128, part * 128 + 128)
        copies.append(pltpu.make_async_copy(gate.at[rows], held_gate.at[rows], sems.at[part]))
    for part in range(2):
        rows = slice(part * 64, part * 64 + 64)
        copies.append(
            pltpu.make_async_copy(hidden.at[rows], held_hidden.at[rows], sems.at[4 + part])
        )
    copies.append(pltpu.make_async_copy(g, held_g, sems.at[6]))
    for copy in copies:
        copy.start()
    for copy in copies[:6]:
        copy.wait()
    logits = jnp.transpose(dot(held_hidden[...], held_gate[...], 1, 0))
    for c in range(2):
        for x in range(4):
            row = x * 64 + c * 32
            partial[c * 4 + x] = logits[row : row + 32]
    copies[6].wait()


def pack_body(q, k, v, g, send, own):
    first = lax.axis_index("core") == 0
    for i, src in enumerate((q, k, v, g)):
        low, high = src[:, :LANES], src[:, LANES:]
        own[i] = jnp.where(first, low, high)
        send[i] = jnp.where(first, high, low)


def pre_body(own, other, state, near_state):
    first = lax.axis_index("core") == 0
    for h in range(HALF):
        lanes = slice(h * DK, (h + 1) * DK)
        state_own = dot(own[1, :, lanes], own[2, :, lanes], 0, 0)
        state_other = dot(other[1, :, lanes], other[2, :, lanes], 0, 0)
        state[h] = (state_own + state_other).astype(BF)
        near_state[h] = (jnp.where(first, state_own, state_other) / SPAN).astype(BF)


def states_body(meta, parts, own, other, state, up, pair, cols, logits, near_grad, chosen):
    core, z, y = meta[0], meta[1], meta[2]
    for s in range(2):
        c = core if s == 0 else 1 - core
        total = parts[c * 4] + parts[c * 4 + 1] + parts[c * 4 + 2] + parts[c * 4 + 3]
        logits[:, s * SPAN : (s + 1) * SPAN] = total
    for h in range(HALF):
        for l in range(8):
            chosen[h * 8 + l : h * 8 + l + 1, :] = logits[pl.ds(h * 8 + meta[3 + l], 1), :]
    x = chosen[...]
    weights = jnp.maximum(x, 0.0) + jnp.log1p(jnp.exp(-jnp.abs(x)))
    padded = jnp.concatenate([weights, jnp.zeros((128 - 8 * HALF, 2 * SPAN), F32)], 0)
    for s in range(2):
        cols[s] = jnp.transpose(padded[:, s * SPAN : (s + 1) * SPAN])
    both = jnp.concatenate([cols[0], cols[1]], 0)
    first = core == 0
    for h in range(HALF):
        lanes = slice(h * DK, (h + 1) * DK)
        q = jnp.concatenate([own[0, :, lanes], other[0, :, lanes]], 0)
        g = jnp.concatenate([own[3, :, lanes], other[3, :, lanes]], 0).astype(F32)
        near = both[:, h * 8 + 1 : h * 8 + 2]
        near_g = (near * g).astype(BF)
        grad_own = dot(q[:SPAN], near_g[:SPAN], 0, 0)
        grad_other = dot(q[SPAN:], near_g[SPAN:], 0, 0)
        near_grad[h] = (jnp.where(first, grad_other, grad_own) / SPAN).astype(BF)
        weighted = jnp.concatenate(
            [(both[:, h * 8 + 2 + i : h * 8 + 3 + i] * g).astype(BF) for i in range(SLOTS)], 1
        )
        grads = dot(q, weighted, 0, 0)
        held = state[h]
        for i in range(SLOTS):
            bit = (z >> i) & 1 if i < 3 else (y >> (i - 3)) & 1
            piece = jnp.where(bit == 1, grads[:, i * DK : (i + 1) * DK].astype(BF), held)
            if i < DIRECT:
                pair[i, h] = piece
            else:
                up[2 * h, i - DIRECT] = piece[:64]
                up[2 * h + 1, i - DIRECT] = piece[64:]


def row_picker(meta, h, levels):
    row = lax.broadcasted_iota(jnp.int32, (8 * HALF, DK), 0)
    return jnp.concatenate(
        [jnp.where(row == h * 8 + meta[3 + l], 1.0, 0.0).astype(BF) for l in levels], 1
    )


def local_body(meta, own, other, cols, near_state, near_grad, part_own, part_other, sums):
    core = meta[0]
    at = lax.broadcasted_iota(jnp.int32, (SPAN, SPAN), 0)
    causal = at >= lax.broadcasted_iota(jnp.int32, (SPAN, SPAN), 1)
    for s, (src, part) in enumerate(((own, part_own), (other, part_other))):
        upper = (core == 1) if s == 0 else (core == 0)
        total = jnp.zeros((8 * HALF, SPAN), F32)
        weights = cols[s]
        for h in range(HALF):
            lanes = slice(h * DK, (h + 1) * DK)
            q, k, v, g = (src[i, :, lanes] for i in range(4))
            gf = g.astype(F32)
            w0 = weights[:, h * 8 : h * 8 + 1]
            w1 = weights[:, h * 8 + 1 : h * 8 + 2]
            g0 = (w0 * gf).astype(BF)
            g1 = (w1 * gf).astype(BF)
            attend = jnp.where(causal, dot(q, k, 1, 1) / SPAN, 0.0).astype(BF)
            score = jnp.where(causal, dot(g0, v, 1, 1) / SPAN, 0.0).astype(BF)
            intra = dot(attend, v, 1, 0)
            zero = jnp.zeros((DK, DK), BF)
            level = jnp.where(upper, near_state[h], zero)
            back = jnp.where(upper, zero, near_grad[h])
            near = dot(q, level, 1, 0)
            part[0, :, lanes] = (w0 * intra + w1 * near).astype(BF)
            part[1, :, lanes] = (dot(score, k, 1, 0) + dot(g1, level, 1, 1)).astype(BF)
            part[2, :, lanes] = (dot(score, q, 0, 0) + dot(v, back, 1, 1)).astype(BF)
            part[3, :, lanes] = (dot(attend, g0, 0, 0) + dot(k, back, 1, 0)).astype(BF)
            products = jnp.concatenate([(gf * intra).astype(BF), (gf * near).astype(BF)], 1)
            total = total + dot(row_picker(meta, h, (0, 1)), products, 1, 1)
        sums[:, s * SPAN : (s + 1) * SPAN] = total


def along_z_body(meta, got, send, halves):
    y = meta[2]
    totals = []
    for i in range(SPREAD - 3, SPREAD):
        total = got[0, i].astype(F32)
        for z in range(1, 8):
            total = total + got[z, i].astype(F32)
        totals.append(total.astype(BF))
    send[y] = jnp.zeros_like(totals[0])
    for step in range(1, 8):
        send[y ^ step] = totals[step.bit_length() - 1]
    for half in range(2):
        total = got[4 * half, 0].astype(F32)
        for z in range(4 * half + 1, 4 * half + 4):
            total = total + got[z, 0].astype(F32)
        halves[half] = (total * (1.0 / (8 * SPAN))).astype(BF)


def pair_body(pair, pair_got, pair_sum):
    for h in range(HALF):
        pair_sum[h] = (pair[1, h].astype(F32) + pair_got[1, h].astype(F32)).astype(BF)


def buckets_body(meta, halves, from_y, pair_got, quad_got, down, direct):
    y = meta[2]
    for z in range(8):
        down[z, 0] = halves[1 - z // 4]
    for i in range(3):
        width = 1 << i
        total = from_y[y ^ width].astype(F32)
        for step in range(width + 1, 2 * width):
            total = total + from_y[y ^ step].astype(F32)
        total = (total * (1.0 / (16 * width * SPAN))).astype(BF)
        for z in range(8):
            down[z, 1 + i] = total
    for h in range(HALF):
        direct[0, h] = pair_got[0, h] * (1.0 / (2 * SPAN))
        direct[1, h] = quad_got[h] * (1.0 / (4 * SPAN))


def level_bits(meta):
    return [(meta[1 + i // 3] >> (i % 3)) & 1 for i in range(SLOTS)]


def bucket_sum(direct, got, h, i):
    if i < DIRECT:
        return direct[i, h]
    return jnp.concatenate([got[2 * h, i - DIRECT], got[2 * h + 1, i - DIRECT]], 0)


def outputs_body(
    meta, own, other, cols, logits, part_own, part_other, sums, direct, got,
    new_own, new_other, logit_grad,
):
    core = meta[0]
    bits = level_bits(meta)
    both = jnp.concatenate([cols[0], cols[1]], 0)
    total = sums[...]
    for h in range(HALF):
        lanes = slice(h * DK, (h + 1) * DK)
        q = jnp.concatenate([own[0, :, lanes], other[0, :, lanes]], 0)
        gf = jnp.concatenate([own[3, :, lanes], other[3, :, lanes]], 0).astype(F32)
        levels = []
        for i in range(SLOTS):
            state = bucket_sum(direct, got, h, i)
            levels.append(jnp.where(bits[i] == 1, state, jnp.zeros_like(state)))
        outs = dot(q, jnp.concatenate(levels, 1), 1, 0)
        mix = jnp.concatenate([part_own[0, :, lanes], part_other[0, :, lanes]], 0).astype(F32)
        products = []
        for i in range(SLOTS):
            out = outs[:, i * DK : (i + 1) * DK]
            mix = mix + both[:, h * 8 + 2 + i : h * 8 + 3 + i] * out
            products.append((gf * out).astype(BF))
        total = total + dot(
            row_picker(meta, h, range(2, 8)), jnp.concatenate(products, 1), 1, 1
        )
        new_own[0, :, lanes] = mix[:SPAN].astype(BF)
        new_other[0, :, lanes] = mix[SPAN:].astype(BF)
    ready = (total * jax.nn.sigmoid(logits[...])).astype(BF)
    for s in range(2):
        c = core if s == 0 else 1 - core
        for x in range(4):
            logit_grad[c * 4 + x] = ready[:, s * SPAN : (s + 1) * SPAN]


def grads_body(meta, own, other, cols, part_own, part_other, direct, got, keep, send):
    bits = level_bits(meta)
    both = jnp.concatenate([cols[0], cols[1]], 0)
    for h in range(HALF):
        lanes = slice(h * DK, (h + 1) * DK)
        k, v, g = (
            jnp.concatenate([own[i, :, lanes], other[i, :, lanes]], 0) for i in range(1, 4)
        )
        gf = g.astype(F32)
        levels, weighted = [], []
        back = jnp.zeros((DK, DK), F32)
        for i in range(SLOTS):
            state = bucket_sum(direct, got, h, i)
            zero = jnp.zeros_like(state)
            levels.append(jnp.where(bits[i] == 1, state, zero))
            back = back + jnp.where(bits[i] == 1, zero, state).astype(F32)
            weighted.append((both[:, h * 8 + 2 + i : h * 8 + 3 + i] * gf).astype(BF))
        back = back.astype(BF)
        found = (
            dot(jnp.concatenate(weighted, 1), jnp.concatenate(levels, 1), 1, 1),
            dot(v, back, 1, 1),
            dot(k, back, 1, 0),
        )
        for s, (part, dst) in enumerate(((part_own, keep), (part_other, send))):
            span = slice(s * SPAN, (s + 1) * SPAN)
            for i in range(3):
                dst[1 + i, :, lanes] = (
                    part[1 + i, :, lanes].astype(F32) + found[i][span]
                ).astype(BF)


def first_body(keep, logit_grad, gate, mixed, dq, dk, dv, dhidden, sems):
    mine = pl.multiple_of(lax.axis_index("core") * LANES, LANES)
    copies = [
        pltpu.make_async_copy(keep.at[i], dst.at[:, pl.ds(mine, LANES)], sems.at[i])
        for i, dst in enumerate((mixed, dq, dk, dv))
    ]
    for copy in copies:
        copy.start()
    grads = jnp.concatenate([logit_grad[c * 4 + x] for x in range(4) for c in range(2)], 0)
    dhidden[...] = dot(grads, gate[...], 0, 1).astype(BF)
    for copy in copies:
        copy.wait()


def second_body(got, old_mixed, old_dq, old_dk, old_dv, mixed, dq, dk, dv, sems):
    theirs = pl.multiple_of((1 - lax.axis_index("core")) * LANES, LANES)
    copies = [
        pltpu.make_async_copy(got.at[i], dst.at[:, pl.ds(theirs, LANES)], sems.at[i])
        for i, dst in enumerate((mixed, dq, dk, dv))
    ]
    for copy in copies:
        copy.start()
    for copy in copies:
        copy.wait()


def local(queries, keys, values, hidden, gate_weight, level_slot, out_grad):
    core, z, y = lax.axis_index("core"), lax.axis_index("z"), lax.axis_index("y")
    place = jnp.stack([core, z, y]).astype(jnp.int32)
    meta = jnp.concatenate([place, level_slot])
    swap = [(0, 1), (1, 0)]

    def exchange(array, axis):
        return lax.all_to_all(array, axis, 0, 0, tiled=True)

    def flip(array, distance):
        return lax.ppermute(array, "z", [(i, i ^ distance) for i in range(8)])

    partial, held_g = pl.pallas_call(
        logits_body,
        out_shape=(shape(8, 32, SPAN, kind=F32), shape(SPAN, 2 * LANES)),
        in_specs=hbm(3),
        out_specs=tuple(vmem(2)),
        scratch_shapes=[
            pltpu.VMEM(hidden.shape, BF),
            pltpu.VMEM(gate_weight.shape, BF),
            pltpu.SemaphoreType.DMA((7,)),
        ],
        compiler_params=SMALL,
        name="logits",
    )(*far(hidden, gate_weight, out_grad))
    parts = exchange(partial, ("core", "head"))
    send, own = pl.pallas_call(
        pack_body,
        out_shape=(shape(4, SPAN, LANES), shape(4, SPAN, LANES)),
        in_specs=vmem(4),
        out_specs=tuple(vmem(2)),
        compiler_params=SMALL,
        name="pack",
    )(*near(queries, keys, values, held_g))
    other = lax.ppermute(send, "core", swap)
    state, near_state = pl.pallas_call(
        pre_body,
        out_shape=(shape(HALF, DK, DK), shape(HALF, DK, DK)),
        in_specs=vmem(2),
        out_specs=tuple(vmem(2)),
        compiler_params=SMALL,
        name="pre",
    )(*near(own, other))
    up, pair, cols, logits, near_grad = pl.pallas_call(
        states_body,
        out_shape=(
            shape(8, SPREAD, 64, DK),
            shape(DIRECT, HALF, DK, DK),
            shape(2, SPAN, 128, kind=F32),
            shape(8 * HALF, 2 * SPAN, kind=F32),
            shape(HALF, DK, DK),
        ),
        in_specs=smem(1) + vmem(4),
        out_specs=tuple(vmem(5)),
        scratch_shapes=[pltpu.VMEM((8 * HALF, 2 * SPAN), F32)],
        compiler_params=SMALL,
        name="states",
    )(meta, *near(parts, own, other, state))
    pair_got = flip(pair, 1)
    got = exchange(up, "z")
    to_y, halves = pl.pallas_call(
        along_z_body,
        out_shape=(shape(8, 64, DK), shape(2, 64, DK)),
        in_specs=smem(1) + vmem(1),
        out_specs=tuple(vmem(2)),
        compiler_params=SMALL,
        name="along_z",
    )(meta, *near(got))
    pair_sum = pl.pallas_call(
        pair_body,
        out_shape=shape(HALF, DK, DK),
        in_specs=vmem(2),
        out_specs=vmem(1)[0],
        compiler_params=SMALL,
        name="pair",
    )(*near(pair, pair_got))
    quad_got = flip(pair_sum, 2)
    from_y = exchange(to_y, "y")
    part_own, part_other, sums = pl.pallas_call(
        local_body,
        out_shape=(
            shape(4, SPAN, LANES),
            shape(4, SPAN, LANES),
            shape(8 * HALF, 2 * SPAN, kind=F32),
        ),
        in_specs=smem(1) + vmem(5),
        out_specs=tuple(vmem(3)),
        compiler_params=SMALL,
        name="local",
    )(meta, *near(own, other, cols, near_state, near_grad))
    down, direct = pl.pallas_call(
        buckets_body,
        out_shape=(shape(8, SPREAD, 64, DK), shape(DIRECT, HALF, DK, DK)),
        in_specs=smem(1) + vmem(4),
        out_specs=tuple(vmem(2)),
        compiler_params=SMALL,
        name="buckets",
    )(meta, *near(halves, from_y, pair_got, quad_got))
    sums_here = exchange(down, "z")
    part_own, part_other, logit_grad = pl.pallas_call(
        outputs_body,
        out_shape=(shape(4, SPAN, LANES), shape(4, SPAN, LANES), shape(8, 8 * HALF, SPAN)),
        in_specs=smem(1) + vmem(9),
        out_specs=tuple(vmem(3)),
        input_output_aliases={5: 0, 6: 1},
        compiler_params=SMALL,
        name="outputs",
    )(meta, *near(own, other, cols, logits, part_own, part_other, sums, direct, sums_here))
    all_grads = exchange(logit_grad, ("core", "head"))
    keep, away = pl.pallas_call(
        grads_body,
        out_shape=(shape(4, SPAN, LANES), shape(4, SPAN, LANES)),
        in_specs=smem(1) + vmem(7),
        out_specs=tuple(vmem(2)),
        input_output_aliases={4: 0, 5: 1},
        compiler_params=SMALL,
        name="grads",
    )(meta, *near(own, other, cols, part_own, part_other, direct, sums_here))
    back = lax.ppermute(away, "core", swap)
    wide = pltpu.HBM((SPAN, 2 * LANES), BF)
    *outs, dhidden = pl.pallas_call(
        first_body,
        out_shape=(wide,) * 4 + (jax.ShapeDtypeStruct((SPAN, hidden.shape[1]), BF),),
        in_specs=vmem(3),
        out_specs=tuple(hbm(4) + vmem(1)),
        scratch_shapes=[pltpu.SemaphoreType.DMA((4,))],
        compiler_params=SMALL,
        name="first",
    )(*near(keep, all_grads), gate_weight)
    outs = pl.pallas_call(
        second_body,
        out_shape=(wide,) * 4,
        in_specs=vmem(1) + hbm(4),
        out_specs=tuple(hbm(4)),
        input_output_aliases={1: 0, 2: 1, 3: 2, 4: 3},
        scratch_shapes=[pltpu.SemaphoreType.DMA((4,))],
        compiler_params=SMALL,
        name="second",
    )(*near(back), *far(*outs))
    return (*outs, dhidden)


def solution(mesh):
    names = ("y", "z", "core", "head")
    fine = Mesh(mesh.devices.reshape(8, 8, 2, 4), names)
    tokens = ("y", "z", "core")
    rows = P(tokens, "head")
    return jax.shard_map(
        local,
        mesh=fine,
        in_specs=(rows, rows, rows, rows, P("head", None), P(), rows),
        out_specs=(rows,) * 5,
        check_vma=False,
    )
```

```python
import jax
import jax.numpy as jnp
from jax import lax
from jax.experimental import pallas as pl
from jax.experimental.pallas import tpu as pltpu
from jax.sharding import Mesh, PartitionSpec as P


DK = 128
SPAN = 128
HALF = 4
LANES = HALF * DK
SLOTS = 6
DIRECT = 2
SPREAD = SLOTS - DIRECT
BF = jnp.bfloat16
F32 = jnp.float32


def dot(a, b, ca, cb):
    return lax.dot_general(a, b, (((ca,), (cb,)), ((), ())), preferred_element_type=F32)


def vmem(n):
    return [pl.BlockSpec(memory_space=pltpu.VMEM)] * n


def hbm(n):
    return [pl.BlockSpec(memory_space=pltpu.HBM)] * n


def smem(n):
    return [pl.BlockSpec(memory_space=pltpu.SMEM)] * n


def shape(*dims, kind=BF):
    return pltpu.VMEM(dims, kind)


def near(*arrays):
    return [pltpu.with_memory_space_constraint(a, pltpu.VMEM) for a in arrays]


def far(*arrays):
    return [pltpu.with_memory_space_constraint(a, pltpu.HBM) for a in arrays]


SMALL = pltpu.CompilerParams(vmem_limit_bytes=16 << 20)


def logits_body(hidden, gate, g, partial, held_g, held_hidden, held_gate, sems):
    copies = []
    for part in range(4):
        rows = slice(part * 128, part * 128 + 128)
        copies.append(pltpu.make_async_copy(gate.at[rows], held_gate.at[rows], sems.at[part]))
    for part in range(2):
        rows = slice(part * 64, part * 64 + 64)
        copies.append(
            pltpu.make_async_copy(hidden.at[rows], held_hidden.at[rows], sems.at[4 + part])
        )
    copies.append(pltpu.make_async_copy(g, held_g, sems.at[6]))
    for copy in copies:
        copy.start()
    for copy in copies[:6]:
        copy.wait()
    logits = jnp.transpose(dot(held_hidden[...], held_gate[...], 1, 0))
    for c in range(2):
        for x in range(4):
            row = x * 64 + c * 32
            partial[c * 4 + x] = logits[row : row + 32]
    copies[6].wait()


def pack_body(q, k, v, g, send, own):
    first = lax.axis_index("core") == 0
    for i, src in enumerate((q, k, v, g)):
        low, high = src[:, :LANES], src[:, LANES:]
        own[i] = jnp.where(first, low, high)
        send[i] = jnp.where(first, high, low)


def pre_body(own, other, state, near_state):
    first = lax.axis_index("core") == 0
    for h in range(HALF):
        lanes = slice(h * DK, (h + 1) * DK)
        state_own = dot(own[1, :, lanes], own[2, :, lanes], 0, 0)
        state_other = dot(other[1, :, lanes], other[2, :, lanes], 0, 0)
        state[h] = (state_own + state_other).astype(BF)
        near_state[h] = (jnp.where(first, state_own, state_other) / SPAN).astype(BF)


def states_body(meta, parts, own, other, state, up, pair, cols, logits, near_grad, chosen):
    core, z, y = meta[0], meta[1], meta[2]
    for s in range(2):
        c = core if s == 0 else 1 - core
        total = parts[c * 4] + parts[c * 4 + 1] + parts[c * 4 + 2] + parts[c * 4 + 3]
        logits[:, s * SPAN : (s + 1) * SPAN] = total
    for h in range(HALF):
        for l in range(8):
            chosen[h * 8 + l : h * 8 + l + 1, :] = logits[pl.ds(h * 8 + meta[3 + l], 1), :]
    x = chosen[...]
    weights = jnp.maximum(x, 0.0) + jnp.log1p(jnp.exp(-jnp.abs(x)))
    padded = jnp.concatenate([weights, jnp.zeros((128 - 8 * HALF, 2 * SPAN), F32)], 0)
    for s in range(2):
        cols[s] = jnp.transpose(padded[:, s * SPAN : (s + 1) * SPAN])
    both = jnp.concatenate([cols[0], cols[1]], 0).astype(BF)
    first = core == 0
    for h in range(HALF):
        lanes = slice(h * DK, (h + 1) * DK)
        q = jnp.concatenate([own[0, :, lanes], other[0, :, lanes]], 0)
        g = jnp.concatenate([own[3, :, lanes], other[3, :, lanes]], 0)
        near = both[:, h * 8 + 1 : h * 8 + 2]
        near_g = near * g
        grad_own = dot(q[:SPAN], near_g[:SPAN], 0, 0)
        grad_other = dot(q[SPAN:], near_g[SPAN:], 0, 0)
        near_grad[h] = (jnp.where(first, grad_other, grad_own) / SPAN).astype(BF)
        weighted = jnp.concatenate(
            [both[:, h * 8 + 2 + i : h * 8 + 3 + i] * g for i in range(SLOTS)], 1
        )
        grads = dot(q, weighted, 0, 0)
        held = state[h]
        for i in range(SLOTS):
            bit = (z >> i) & 1 if i < 3 else (y >> (i - 3)) & 1
            piece = jnp.where(bit == 1, grads[:, i * DK : (i + 1) * DK].astype(BF), held)
            if i < DIRECT:
                pair[i, h] = piece
            else:
                up[2 * h, i - DIRECT] = piece[:64]
                up[2 * h + 1, i - DIRECT] = piece[64:]


def row_picker(meta, h, levels):
    row = lax.broadcasted_iota(jnp.int32, (8 * HALF, DK), 0)
    return jnp.concatenate(
        [jnp.where(row == h * 8 + meta[3 + l], 1.0, 0.0).astype(BF) for l in levels], 1
    )


def local_body(meta, own, other, cols, near_state, near_grad, part_own, part_other, sums):
    core = meta[0]
    at = lax.broadcasted_iota(jnp.int32, (SPAN, SPAN), 0)
    causal = at >= lax.broadcasted_iota(jnp.int32, (SPAN, SPAN), 1)
    for s, (src, part) in enumerate(((own, part_own), (other, part_other))):
        upper = (core == 1) if s == 0 else (core == 0)
        total = jnp.zeros((8 * HALF, SPAN), F32)
        weights = cols[s]
        for h in range(HALF):
            lanes = slice(h * DK, (h + 1) * DK)
            q, k, v, g = (src[i, :, lanes] for i in range(4))
            gf = g.astype(F32)
            w0 = weights[:, h * 8 : h * 8 + 1]
            w1 = weights[:, h * 8 + 1 : h * 8 + 2]
            g0 = (w0 * gf).astype(BF)
            g1 = (w1 * gf).astype(BF)
            attend = jnp.where(causal, dot(q, k, 1, 1) / SPAN, 0.0).astype(BF)
            score = jnp.where(causal, dot(g0, v, 1, 1) / SPAN, 0.0).astype(BF)
            intra = dot(attend, v, 1, 0)
            zero = jnp.zeros((DK, DK), BF)
            level = jnp.where(upper, near_state[h], zero)
            back = jnp.where(upper, zero, near_grad[h])
            near = dot(q, level, 1, 0)
            part[0, :, lanes] = (w0 * intra + w1 * near).astype(BF)
            part[1, :, lanes] = (dot(score, k, 1, 0) + dot(g1, level, 1, 1)).astype(BF)
            part[2, :, lanes] = (dot(score, q, 0, 0) + dot(v, back, 1, 1)).astype(BF)
            part[3, :, lanes] = (dot(attend, g0, 0, 0) + dot(k, back, 1, 0)).astype(BF)
            products = jnp.concatenate([(gf * intra).astype(BF), (gf * near).astype(BF)], 1)
            total = total + dot(row_picker(meta, h, (0, 1)), products, 1, 1)
        sums[:, s * SPAN : (s + 1) * SPAN] = total


def along_z_body(meta, got, send, halves):
    y = meta[2]
    totals = []
    for i in range(SPREAD - 3, SPREAD):
        total = got[0, i].astype(F32)
        for z in range(1, 8):
            total = total + got[z, i].astype(F32)
        totals.append(total.astype(BF))
    send[y] = jnp.zeros_like(totals[0])
    for step in range(1, 8):
        send[y ^ step] = totals[step.bit_length() - 1]
    for half in range(2):
        total = got[4 * half, 0].astype(F32)
        for z in range(4 * half + 1, 4 * half + 4):
            total = total + got[z, 0].astype(F32)
        halves[half] = (total * (1.0 / (8 * SPAN))).astype(BF)


def pair_body(pair, pair_got, pair_sum):
    for h in range(HALF):
        pair_sum[h] = (pair[1, h].astype(F32) + pair_got[1, h].astype(F32)).astype(BF)


def buckets_body(meta, halves, from_y, pair_got, quad_got, down, direct):
    y = meta[2]
    for z in range(8):
        down[z, 0] = halves[1 - z // 4]
    for i in range(3):
        width = 1 << i
        total = from_y[y ^ width].astype(F32)
        for step in range(width + 1, 2 * width):
            total = total + from_y[y ^ step].astype(F32)
        total = (total * (1.0 / (16 * width * SPAN))).astype(BF)
        for z in range(8):
            down[z, 1 + i] = total
    for h in range(HALF):
        direct[0, h] = pair_got[0, h] * (1.0 / (2 * SPAN))
        direct[1, h] = quad_got[h] * (1.0 / (4 * SPAN))


def level_bits(meta):
    return [(meta[1 + i // 3] >> (i % 3)) & 1 for i in range(SLOTS)]


def bucket_sum(direct, got, h, i):
    if i < DIRECT:
        return direct[i, h]
    return jnp.concatenate([got[2 * h, i - DIRECT], got[2 * h + 1, i - DIRECT]], 0)


def outputs_body(
    meta, own, other, cols, logits, part_own, part_other, sums, direct, got,
    new_own, new_other, logit_grad,
):
    core = meta[0]
    bits = level_bits(meta)
    both = jnp.concatenate([cols[0], cols[1]], 0)
    total = sums[...]
    for h in range(HALF):
        lanes = slice(h * DK, (h + 1) * DK)
        q = jnp.concatenate([own[0, :, lanes], other[0, :, lanes]], 0)
        gf = jnp.concatenate([own[3, :, lanes], other[3, :, lanes]], 0).astype(F32)
        levels = []
        for i in range(SLOTS):
            state = bucket_sum(direct, got, h, i)
            levels.append(jnp.where(bits[i] == 1, state, jnp.zeros_like(state)))
        outs = dot(q, jnp.concatenate(levels, 1), 1, 0)
        mix = jnp.concatenate([part_own[0, :, lanes], part_other[0, :, lanes]], 0).astype(F32)
        products = []
        for i in range(SLOTS):
            out = outs[:, i * DK : (i + 1) * DK]
            mix = mix + both[:, h * 8 + 2 + i : h * 8 + 3 + i] * out
            products.append((gf * out).astype(BF))
        total = total + dot(
            row_picker(meta, h, range(2, 8)), jnp.concatenate(products, 1), 1, 1
        )
        new_own[0, :, lanes] = mix[:SPAN].astype(BF)
        new_other[0, :, lanes] = mix[SPAN:].astype(BF)
    ready = (total * jax.nn.sigmoid(logits[...])).astype(BF)
    for s in range(2):
        c = core if s == 0 else 1 - core
        for x in range(4):
            logit_grad[c * 4 + x] = ready[:, s * SPAN : (s + 1) * SPAN]


def grads_body(meta, own, other, cols, part_own, part_other, direct, got, keep, send):
    bits = level_bits(meta)
    both = jnp.concatenate([cols[0], cols[1]], 0).astype(BF)
    for h in range(HALF):
        lanes = slice(h * DK, (h + 1) * DK)
        k, v, g = (
            jnp.concatenate([own[i, :, lanes], other[i, :, lanes]], 0) for i in range(1, 4)
        )
        levels, weighted = [], []
        back = jnp.zeros((DK, DK), F32)
        for i in range(SLOTS):
            state = bucket_sum(direct, got, h, i)
            zero = jnp.zeros_like(state)
            levels.append(jnp.where(bits[i] == 1, state, zero))
            back = back + jnp.where(bits[i] == 1, zero, state).astype(F32)
            weighted.append(both[:, h * 8 + 2 + i : h * 8 + 3 + i] * g)
        back = back.astype(BF)
        found = (
            dot(jnp.concatenate(weighted, 1), jnp.concatenate(levels, 1), 1, 1),
            dot(v, back, 1, 1),
            dot(k, back, 1, 0),
        )
        for s, (part, dst) in enumerate(((part_own, keep), (part_other, send))):
            span = slice(s * SPAN, (s + 1) * SPAN)
            for i in range(3):
                dst[1 + i, :, lanes] = (
                    part[1 + i, :, lanes].astype(F32) + found[i][span]
                ).astype(BF)


def first_body(keep, logit_grad, gate, mixed, dq, dk, dv, dhidden, sems):
    mine = pl.multiple_of(lax.axis_index("core") * LANES, LANES)
    copies = [
        pltpu.make_async_copy(keep.at[i], dst.at[:, pl.ds(mine, LANES)], sems.at[i])
        for i, dst in enumerate((mixed, dq, dk, dv))
    ]
    for copy in copies:
        copy.start()
    grads = jnp.concatenate([logit_grad[c * 4 + x] for x in range(4) for c in range(2)], 0)
    dhidden[...] = dot(grads, gate[...], 0, 1).astype(BF)
    for copy in copies:
        copy.wait()


def second_body(got, old_mixed, old_dq, old_dk, old_dv, mixed, dq, dk, dv, sems):
    theirs = pl.multiple_of((1 - lax.axis_index("core")) * LANES, LANES)
    copies = [
        pltpu.make_async_copy(got.at[i], dst.at[:, pl.ds(theirs, LANES)], sems.at[i])
        for i, dst in enumerate((mixed, dq, dk, dv))
    ]
    for copy in copies:
        copy.start()
    for copy in copies:
        copy.wait()


def local(queries, keys, values, hidden, gate_weight, level_slot, out_grad):
    core, z, y = lax.axis_index("core"), lax.axis_index("z"), lax.axis_index("y")
    place = jnp.stack([core, z, y]).astype(jnp.int32)
    meta = jnp.concatenate([place, level_slot])
    swap = [(0, 1), (1, 0)]

    def exchange(array, axis):
        return lax.all_to_all(array, axis, 0, 0, tiled=True)

    def flip(array, distance):
        return lax.ppermute(array, "z", [(i, i ^ distance) for i in range(8)])

    partial, held_g = pl.pallas_call(
        logits_body,
        out_shape=(shape(8, 32, SPAN, kind=F32), shape(SPAN, 2 * LANES)),
        in_specs=hbm(3),
        out_specs=tuple(vmem(2)),
        scratch_shapes=[
            pltpu.VMEM(hidden.shape, BF),
            pltpu.VMEM(gate_weight.shape, BF),
            pltpu.SemaphoreType.DMA((7,)),
        ],
        compiler_params=SMALL,
        name="logits",
    )(*far(hidden, gate_weight, out_grad))
    parts = exchange(partial, ("core", "head"))
    send, own = pl.pallas_call(
        pack_body,
        out_shape=(shape(4, SPAN, LANES), shape(4, SPAN, LANES)),
        in_specs=vmem(4),
        out_specs=tuple(vmem(2)),
        compiler_params=SMALL,
        name="pack",
    )(*near(queries, keys, values, held_g))
    other = lax.ppermute(send, "core", swap)
    state, near_state = pl.pallas_call(
        pre_body,
        out_shape=(shape(HALF, DK, DK), shape(HALF, DK, DK)),
        in_specs=vmem(2),
        out_specs=tuple(vmem(2)),
        compiler_params=SMALL,
        name="pre",
    )(*near(own, other))
    up, pair, cols, logits, near_grad = pl.pallas_call(
        states_body,
        out_shape=(
            shape(8, SPREAD, 64, DK),
            shape(DIRECT, HALF, DK, DK),
            shape(2, SPAN, 128, kind=F32),
            shape(8 * HALF, 2 * SPAN, kind=F32),
            shape(HALF, DK, DK),
        ),
        in_specs=smem(1) + vmem(4),
        out_specs=tuple(vmem(5)),
        scratch_shapes=[pltpu.VMEM((8 * HALF, 2 * SPAN), F32)],
        compiler_params=SMALL,
        name="states",
    )(meta, *near(parts, own, other, state))
    pair_got = flip(pair, 1)
    got = exchange(up, "z")
    to_y, halves = pl.pallas_call(
        along_z_body,
        out_shape=(shape(8, 64, DK), shape(2, 64, DK)),
        in_specs=smem(1) + vmem(1),
        out_specs=tuple(vmem(2)),
        compiler_params=SMALL,
        name="along_z",
    )(meta, *near(got))
    pair_sum = pl.pallas_call(
        pair_body,
        out_shape=shape(HALF, DK, DK),
        in_specs=vmem(2),
        out_specs=vmem(1)[0],
        compiler_params=SMALL,
        name="pair",
    )(*near(pair, pair_got))
    quad_got = flip(pair_sum, 2)
    from_y = exchange(to_y, "y")
    part_own, part_other, sums = pl.pallas_call(
        local_body,
        out_shape=(
            shape(4, SPAN, LANES),
            shape(4, SPAN, LANES),
            shape(8 * HALF, 2 * SPAN, kind=F32),
        ),
        in_specs=smem(1) + vmem(5),
        out_specs=tuple(vmem(3)),
        compiler_params=SMALL,
        name="local",
    )(meta, *near(own, other, cols, near_state, near_grad))
    down, direct = pl.pallas_call(
        buckets_body,
        out_shape=(shape(8, SPREAD, 64, DK), shape(DIRECT, HALF, DK, DK)),
        in_specs=smem(1) + vmem(4),
        out_specs=tuple(vmem(2)),
        compiler_params=SMALL,
        name="buckets",
    )(meta, *near(halves, from_y, pair_got, quad_got))
    sums_here = exchange(down, "z")
    part_own, part_other, logit_grad = pl.pallas_call(
        outputs_body,
        out_shape=(shape(4, SPAN, LANES), shape(4, SPAN, LANES), shape(8, 8 * HALF, SPAN)),
        in_specs=smem(1) + vmem(9),
        out_specs=tuple(vmem(3)),
        input_output_aliases={5: 0, 6: 1},
        compiler_params=SMALL,
        name="outputs",
    )(meta, *near(own, other, cols, logits, part_own, part_other, sums, direct, sums_here))
    all_grads = exchange(logit_grad, ("core", "head"))
    keep, away = pl.pallas_call(
        grads_body,
        out_shape=(shape(4, SPAN, LANES), shape(4, SPAN, LANES)),
        in_specs=smem(1) + vmem(7),
        out_specs=tuple(vmem(2)),
        input_output_aliases={4: 0, 5: 1},
        compiler_params=SMALL,
        name="grads",
    )(meta, *near(own, other, cols, part_own, part_other, direct, sums_here))
    back = lax.ppermute(away, "core", swap)
    wide = pltpu.HBM((SPAN, 2 * LANES), BF)
    *outs, dhidden = pl.pallas_call(
        first_body,
        out_shape=(wide,) * 4 + (jax.ShapeDtypeStruct((SPAN, hidden.shape[1]), BF),),
        in_specs=vmem(3),
        out_specs=tuple(hbm(4) + vmem(1)),
        scratch_shapes=[pltpu.SemaphoreType.DMA((4,))],
        compiler_params=SMALL,
        name="first",
    )(*near(keep, all_grads), gate_weight)
    outs = pl.pallas_call(
        second_body,
        out_shape=(wide,) * 4,
        in_specs=vmem(1) + hbm(4),
        out_specs=tuple(hbm(4)),
        input_output_aliases={1: 0, 2: 1, 3: 2, 4: 3},
        scratch_shapes=[pltpu.SemaphoreType.DMA((4,))],
        compiler_params=SMALL,
        name="second",
    )(*near(back), *far(*outs))
    return (*outs, dhidden)


def solution(mesh):
    names = ("y", "z", "core", "head")
    fine = Mesh(mesh.devices.reshape(8, 8, 2, 4), names)
    tokens = ("y", "z", "core")
    rows = P(tokens, "head")
    return jax.shard_map(
        local,
        mesh=fine,
        in_specs=(rows, rows, rows, rows, P("head", None), P(), rows),
        out_specs=(rows,) * 5,
        check_vma=False,
    )
```

```python
import jax
import jax.numpy as jnp
from jax import lax
from jax.experimental import pallas as pl
from jax.experimental.pallas import tpu as pltpu
from jax.sharding import Mesh, PartitionSpec as P


DK = 128
SPAN = 128
HALF = 4
LANES = HALF * DK
SLOTS = 6
DIRECT = 2
SPREAD = SLOTS - DIRECT
BF = jnp.bfloat16
F32 = jnp.float32


def dot(a, b, ca, cb):
    return lax.dot_general(a, b, (((ca,), (cb,)), ((), ())), preferred_element_type=F32)


def vmem(n):
    return [pl.BlockSpec(memory_space=pltpu.VMEM)] * n


def hbm(n):
    return [pl.BlockSpec(memory_space=pltpu.HBM)] * n


def smem(n):
    return [pl.BlockSpec(memory_space=pltpu.SMEM)] * n


def shape(*dims, kind=BF):
    return pltpu.VMEM(dims, kind)


def near(*arrays):
    return [pltpu.with_memory_space_constraint(a, pltpu.VMEM) for a in arrays]


def far(*arrays):
    return [pltpu.with_memory_space_constraint(a, pltpu.HBM) for a in arrays]


SMALL = pltpu.CompilerParams(vmem_limit_bytes=16 << 20)


def logits_body(hidden, gate, g, partial, held_g, held_hidden, held_gate, sems):
    copies = []
    for part in range(4):
        rows = slice(part * 128, part * 128 + 128)
        copies.append(pltpu.make_async_copy(gate.at[rows], held_gate.at[rows], sems.at[part]))
    for part in range(2):
        rows = slice(part * 64, part * 64 + 64)
        copies.append(
            pltpu.make_async_copy(hidden.at[rows], held_hidden.at[rows], sems.at[4 + part])
        )
    copies.append(pltpu.make_async_copy(g, held_g, sems.at[6]))
    for copy in copies:
        copy.start()
    for copy in copies[:6]:
        copy.wait()
    logits = jnp.transpose(dot(held_hidden[...], held_gate[...], 1, 0))
    for c in range(2):
        for x in range(4):
            row = x * 64 + c * 32
            partial[c * 4 + x] = logits[row : row + 32]
    copies[6].wait()


def pack_body(q, k, v, g, send, own):
    first = lax.axis_index("core") == 0
    for i, src in enumerate((q, k, v, g)):
        low, high = src[:, :LANES], src[:, LANES:]
        own[i] = jnp.where(first, low, high)
        send[i] = jnp.where(first, high, low)


def pre_body(own, other, state, near_state):
    first = lax.axis_index("core") == 0
    for h in range(HALF):
        lanes = slice(h * DK, (h + 1) * DK)
        state_own = dot(own[1, :, lanes], own[2, :, lanes], 0, 0)
        state_other = dot(other[1, :, lanes], other[2, :, lanes], 0, 0)
        state[h] = (state_own + state_other).astype(BF)
        near_state[h] = (jnp.where(first, state_own, state_other) / SPAN).astype(BF)


def states_body(meta, parts, own, other, state, up, pair, cols, logits, near_grad, chosen):
    core, z, y = meta[0], meta[1], meta[2]
    for s in range(2):
        c = core if s == 0 else 1 - core
        total = parts[c * 4] + parts[c * 4 + 1] + parts[c * 4 + 2] + parts[c * 4 + 3]
        logits[:, s * SPAN : (s + 1) * SPAN] = total
    for h in range(HALF):
        for l in range(8):
            chosen[h * 8 + l : h * 8 + l + 1, :] = logits[pl.ds(h * 8 + meta[3 + l], 1), :]
    x = chosen[...]
    weights = jnp.maximum(x, 0.0) + jnp.log1p(jnp.exp(-jnp.abs(x)))
    padded = jnp.concatenate([weights, jnp.zeros((128 - 8 * HALF, 2 * SPAN), F32)], 0)
    for s in range(2):
        cols[s] = jnp.transpose(padded[:, s * SPAN : (s + 1) * SPAN])
    both = jnp.concatenate([cols[0], cols[1]], 0).astype(BF)
    first = core == 0
    for h in range(HALF):
        lanes = slice(h * DK, (h + 1) * DK)
        q = jnp.concatenate([own[0, :, lanes], other[0, :, lanes]], 0)
        g = jnp.concatenate([own[3, :, lanes], other[3, :, lanes]], 0)
        near = both[:, h * 8 + 1 : h * 8 + 2]
        near_g = near * g
        grad_own = dot(q[:SPAN], near_g[:SPAN], 0, 0)
        grad_other = dot(q[SPAN:], near_g[SPAN:], 0, 0)
        near_grad[h] = (jnp.where(first, grad_other, grad_own) / SPAN).astype(BF)
        weighted = jnp.concatenate(
            [both[:, h * 8 + 2 + i : h * 8 + 3 + i] * g for i in range(SLOTS)], 1
        )
        grads = dot(q, weighted, 0, 0)
        held = state[h]
        for i in range(SLOTS):
            bit = (z >> i) & 1 if i < 3 else (y >> (i - 3)) & 1
            piece = jnp.where(bit == 1, grads[:, i * DK : (i + 1) * DK].astype(BF), held)
            if i < DIRECT:
                pair[i, h] = piece
            else:
                up[2 * h, i - DIRECT] = piece[:64]
                up[2 * h + 1, i - DIRECT] = piece[64:]


def row_picker(meta, h, levels):
    row = lax.broadcasted_iota(jnp.int32, (8 * HALF, DK), 0)
    return jnp.concatenate(
        [jnp.where(row == h * 8 + meta[3 + l], 1.0, 0.0).astype(BF) for l in levels], 1
    )


def local_body(meta, own, other, cols, near_state, near_grad, part_own, part_other, sums):
    core = meta[0]
    at = lax.broadcasted_iota(jnp.int32, (SPAN, SPAN), 0)
    causal = at >= lax.broadcasted_iota(jnp.int32, (SPAN, SPAN), 1)
    for s, (src, part) in enumerate(((own, part_own), (other, part_other))):
        upper = (core == 1) if s == 0 else (core == 0)
        total = jnp.zeros((8 * HALF, SPAN), F32)
        weights = cols[s]
        for h in range(HALF):
            lanes = slice(h * DK, (h + 1) * DK)
            q, k, v, g = (src[i, :, lanes] for i in range(4))
            gf = g.astype(F32)
            w0 = weights[:, h * 8 : h * 8 + 1]
            w1 = weights[:, h * 8 + 1 : h * 8 + 2]
            g0 = (w0 * gf).astype(BF)
            g1 = (w1 * gf).astype(BF)
            attend = jnp.where(causal, dot(q, k, 1, 1) / SPAN, 0.0).astype(BF)
            score = jnp.where(causal, dot(g0, v, 1, 1) / SPAN, 0.0).astype(BF)
            intra = dot(attend, v, 1, 0)
            zero = jnp.zeros((DK, DK), BF)
            level = jnp.where(upper, near_state[h], zero)
            back = jnp.where(upper, zero, near_grad[h])
            near = dot(q, level, 1, 0)
            part[0, :, lanes] = (w0 * intra + w1 * near).astype(BF)
            part[1, :, lanes] = (dot(score, k, 1, 0) + dot(g1, level, 1, 1)).astype(BF)
            part[2, :, lanes] = (dot(score, q, 0, 0) + dot(v, back, 1, 1)).astype(BF)
            part[3, :, lanes] = (dot(attend, g0, 0, 0) + dot(k, back, 1, 0)).astype(BF)
            products = jnp.concatenate([(gf * intra).astype(BF), (gf * near).astype(BF)], 1)
            total = total + dot(row_picker(meta, h, (0, 1)), products, 1, 1)
        sums[:, s * SPAN : (s + 1) * SPAN] = total


def along_z_body(meta, got, send, halves):
    y = meta[2]
    totals = []
    for i in range(SPREAD - 3, SPREAD):
        total = got[0, i].astype(F32)
        for z in range(1, 8):
            total = total + got[z, i].astype(F32)
        totals.append(total.astype(BF))
    send[y] = jnp.zeros_like(totals[0])
    for step in range(1, 8):
        send[y ^ step] = totals[step.bit_length() - 1]
    for half in range(2):
        total = got[4 * half, 0].astype(F32)
        for z in range(4 * half + 1, 4 * half + 4):
            total = total + got[z, 0].astype(F32)
        halves[half] = (total * (1.0 / (8 * SPAN))).astype(BF)


def pair_body(pair, pair_got, pair_sum):
    for h in range(HALF):
        pair_sum[h] = (pair[1, h].astype(F32) + pair_got[1, h].astype(F32)).astype(BF)


def buckets_body(meta, halves, from_y, pair_got, quad_got, down, direct):
    y = meta[2]
    for z in range(8):
        down[z, 0] = halves[1 - z // 4]
    for i in range(3):
        width = 1 << i
        total = from_y[y ^ width].astype(F32)
        for step in range(width + 1, 2 * width):
            total = total + from_y[y ^ step].astype(F32)
        total = (total * (1.0 / (16 * width * SPAN))).astype(BF)
        for z in range(8):
            down[z, 1 + i] = total
    for h in range(HALF):
        direct[0, h] = pair_got[0, h] * (1.0 / (2 * SPAN))
        direct[1, h] = quad_got[h] * (1.0 / (4 * SPAN))


def level_bits(meta):
    return [(meta[1 + i // 3] >> (i % 3)) & 1 for i in range(SLOTS)]


def bucket_sum(direct, got, h, i):
    if i < DIRECT:
        return direct[i, h]
    return jnp.concatenate([got[2 * h, i - DIRECT], got[2 * h + 1, i - DIRECT]], 0)


def outputs_body(
    meta, own, other, cols, logits, part_own, part_other, sums, direct, got,
    new_own, new_other, logit_grad,
):
    core = meta[0]
    bits = level_bits(meta)
    both = jnp.concatenate([cols[0], cols[1]], 0).astype(BF)
    total = sums[...]
    for h in range(HALF):
        lanes = slice(h * DK, (h + 1) * DK)
        q = jnp.concatenate([own[0, :, lanes], other[0, :, lanes]], 0)
        gf = jnp.concatenate([own[3, :, lanes], other[3, :, lanes]], 0).astype(F32)
        levels = []
        for i in range(SLOTS):
            state = bucket_sum(direct, got, h, i)
            levels.append(jnp.where(bits[i] == 1, state, jnp.zeros_like(state)))
        outs = dot(q, jnp.concatenate(levels, 1), 1, 0)
        mix = jnp.concatenate([part_own[0, :, lanes], part_other[0, :, lanes]], 0).astype(F32)
        products = []
        for i in range(SLOTS):
            out = outs[:, i * DK : (i + 1) * DK]
            wide = jnp.broadcast_to(both[:, h * 8 + 2 + i : h * 8 + 3 + i], (2 * SPAN, DK))
            mix = mix + wide.astype(F32) * out
            products.append((gf * out).astype(BF))
        total = total + dot(
            row_picker(meta, h, range(2, 8)), jnp.concatenate(products, 1), 1, 1
        )
        new_own[0, :, lanes] = mix[:SPAN].astype(BF)
        new_other[0, :, lanes] = mix[SPAN:].astype(BF)
    ready = (total * jax.nn.sigmoid(logits[...])).astype(BF)
    for s in range(2):
        c = core if s == 0 else 1 - core
        for x in range(4):
            logit_grad[c * 4 + x] = ready[:, s * SPAN : (s + 1) * SPAN]


def grads_body(meta, own, other, cols, part_own, part_other, direct, got, keep, send):
    bits = level_bits(meta)
    both = jnp.concatenate([cols[0], cols[1]], 0).astype(BF)
    for h in range(HALF):
        lanes = slice(h * DK, (h + 1) * DK)
        k, v, g = (
            jnp.concatenate([own[i, :, lanes], other[i, :, lanes]], 0) for i in range(1, 4)
        )
        levels, weighted = [], []
        back = jnp.zeros((DK, DK), F32)
        for i in range(SLOTS):
            state = bucket_sum(direct, got, h, i)
            zero = jnp.zeros_like(state)
            levels.append(jnp.where(bits[i] == 1, state, zero))
            back = back + jnp.where(bits[i] == 1, zero, state).astype(F32)
            weighted.append(both[:, h * 8 + 2 + i : h * 8 + 3 + i] * g)
        back = back.astype(BF)
        found = (
            dot(jnp.concatenate(weighted, 1), jnp.concatenate(levels, 1), 1, 1),
            dot(v, back, 1, 1),
            dot(k, back, 1, 0),
        )
        for s, (part, dst) in enumerate(((part_own, keep), (part_other, send))):
            span = slice(s * SPAN, (s + 1) * SPAN)
            for i in range(3):
                dst[1 + i, :, lanes] = (
                    part[1 + i, :, lanes].astype(F32) + found[i][span]
                ).astype(BF)


def first_body(keep, logit_grad, gate, mixed, dq, dk, dv, dhidden, sems):
    mine = pl.multiple_of(lax.axis_index("core") * LANES, LANES)
    copies = [
        pltpu.make_async_copy(keep.at[i], dst.at[:, pl.ds(mine, LANES)], sems.at[i])
        for i, dst in enumerate((mixed, dq, dk, dv))
    ]
    for copy in copies:
        copy.start()
    grads = jnp.concatenate([logit_grad[c * 4 + x] for x in range(4) for c in range(2)], 0)
    dhidden[...] = dot(grads, gate[...], 0, 1).astype(BF)
    for copy in copies:
        copy.wait()


def second_body(got, old_mixed, old_dq, old_dk, old_dv, mixed, dq, dk, dv, sems):
    theirs = pl.multiple_of((1 - lax.axis_index("core")) * LANES, LANES)
    copies = [
        pltpu.make_async_copy(got.at[i], dst.at[:, pl.ds(theirs, LANES)], sems.at[i])
        for i, dst in enumerate((mixed, dq, dk, dv))
    ]
    for copy in copies:
        copy.start()
    for copy in copies:
        copy.wait()


def local(queries, keys, values, hidden, gate_weight, level_slot, out_grad):
    core, z, y = lax.axis_index("core"), lax.axis_index("z"), lax.axis_index("y")
    place = jnp.stack([core, z, y]).astype(jnp.int32)
    meta = jnp.concatenate([place, level_slot])
    swap = [(0, 1), (1, 0)]

    def exchange(array, axis):
        return lax.all_to_all(array, axis, 0, 0, tiled=True)

    def flip(array, distance):
        return lax.ppermute(array, "z", [(i, i ^ distance) for i in range(8)])

    partial, held_g = pl.pallas_call(
        logits_body,
        out_shape=(shape(8, 32, SPAN, kind=F32), shape(SPAN, 2 * LANES)),
        in_specs=hbm(3),
        out_specs=tuple(vmem(2)),
        scratch_shapes=[
            pltpu.VMEM(hidden.shape, BF),
            pltpu.VMEM(gate_weight.shape, BF),
            pltpu.SemaphoreType.DMA((7,)),
        ],
        compiler_params=SMALL,
        name="logits",
    )(*far(hidden, gate_weight, out_grad))
    parts = exchange(partial, ("core", "head"))
    send, own = pl.pallas_call(
        pack_body,
        out_shape=(shape(4, SPAN, LANES), shape(4, SPAN, LANES)),
        in_specs=vmem(4),
        out_specs=tuple(vmem(2)),
        compiler_params=SMALL,
        name="pack",
    )(*near(queries, keys, values, held_g))
    other = lax.ppermute(send, "core", swap)
    state, near_state = pl.pallas_call(
        pre_body,
        out_shape=(shape(HALF, DK, DK), shape(HALF, DK, DK)),
        in_specs=vmem(2),
        out_specs=tuple(vmem(2)),
        compiler_params=SMALL,
        name="pre",
    )(*near(own, other))
    up, pair, cols, logits, near_grad = pl.pallas_call(
        states_body,
        out_shape=(
            shape(8, SPREAD, 64, DK),
            shape(DIRECT, HALF, DK, DK),
            shape(2, SPAN, 128, kind=F32),
            shape(8 * HALF, 2 * SPAN, kind=F32),
            shape(HALF, DK, DK),
        ),
        in_specs=smem(1) + vmem(4),
        out_specs=tuple(vmem(5)),
        scratch_shapes=[pltpu.VMEM((8 * HALF, 2 * SPAN), F32)],
        compiler_params=SMALL,
        name="states",
    )(meta, *near(parts, own, other, state))
    pair_got = flip(pair, 1)
    got = exchange(up, "z")
    to_y, halves = pl.pallas_call(
        along_z_body,
        out_shape=(shape(8, 64, DK), shape(2, 64, DK)),
        in_specs=smem(1) + vmem(1),
        out_specs=tuple(vmem(2)),
        compiler_params=SMALL,
        name="along_z",
    )(meta, *near(got))
    pair_sum = pl.pallas_call(
        pair_body,
        out_shape=shape(HALF, DK, DK),
        in_specs=vmem(2),
        out_specs=vmem(1)[0],
        compiler_params=SMALL,
        name="pair",
    )(*near(pair, pair_got))
    quad_got = flip(pair_sum, 2)
    from_y = exchange(to_y, "y")
    part_own, part_other, sums = pl.pallas_call(
        local_body,
        out_shape=(
            shape(4, SPAN, LANES),
            shape(4, SPAN, LANES),
            shape(8 * HALF, 2 * SPAN, kind=F32),
        ),
        in_specs=smem(1) + vmem(5),
        out_specs=tuple(vmem(3)),
        compiler_params=SMALL,
        name="local",
    )(meta, *near(own, other, cols, near_state, near_grad))
    down, direct = pl.pallas_call(
        buckets_body,
        out_shape=(shape(8, SPREAD, 64, DK), shape(DIRECT, HALF, DK, DK)),
        in_specs=smem(1) + vmem(4),
        out_specs=tuple(vmem(2)),
        compiler_params=SMALL,
        name="buckets",
    )(meta, *near(halves, from_y, pair_got, quad_got))
    sums_here = exchange(down, "z")
    part_own, part_other, logit_grad = pl.pallas_call(
        outputs_body,
        out_shape=(shape(4, SPAN, LANES), shape(4, SPAN, LANES), shape(8, 8 * HALF, SPAN)),
        in_specs=smem(1) + vmem(9),
        out_specs=tuple(vmem(3)),
        input_output_aliases={5: 0, 6: 1},
        compiler_params=SMALL,
        name="outputs",
    )(meta, *near(own, other, cols, logits, part_own, part_other, sums, direct, sums_here))
    all_grads = exchange(logit_grad, ("core", "head"))
    keep, away = pl.pallas_call(
        grads_body,
        out_shape=(shape(4, SPAN, LANES), shape(4, SPAN, LANES)),
        in_specs=smem(1) + vmem(7),
        out_specs=tuple(vmem(2)),
        input_output_aliases={4: 0, 5: 1},
        compiler_params=SMALL,
        name="grads",
    )(meta, *near(own, other, cols, part_own, part_other, direct, sums_here))
    back = lax.ppermute(away, "core", swap)
    wide = pltpu.HBM((SPAN, 2 * LANES), BF)
    *outs, dhidden = pl.pallas_call(
        first_body,
        out_shape=(wide,) * 4 + (jax.ShapeDtypeStruct((SPAN, hidden.shape[1]), BF),),
        in_specs=vmem(3),
        out_specs=tuple(hbm(4) + vmem(1)),
        scratch_shapes=[pltpu.SemaphoreType.DMA((4,))],
        compiler_params=SMALL,
        name="first",
    )(*near(keep, all_grads), gate_weight)
    outs = pl.pallas_call(
        second_body,
        out_shape=(wide,) * 4,
        in_specs=vmem(1) + hbm(4),
        out_specs=tuple(hbm(4)),
        input_output_aliases={1: 0, 2: 1, 3: 2, 4: 3},
        scratch_shapes=[pltpu.SemaphoreType.DMA((4,))],
        compiler_params=SMALL,
        name="second",
    )(*near(back), *far(*outs))
    return (*outs, dhidden)


def solution(mesh):
    names = ("y", "z", "core", "head")
    fine = Mesh(mesh.devices.reshape(8, 8, 2, 4), names)
    tokens = ("y", "z", "core")
    rows = P(tokens, "head")
    return jax.shard_map(
        local,
        mesh=fine,
        in_specs=(rows, rows, rows, rows, P("head", None), P(), rows),
        out_specs=(rows,) * 5,
        check_vma=False,
    )
```
